128 devices in a mesh: dp: 32 (over x, z, y_lo), frame: 4 (over y_hi, core).
Axes of the slice: x: 4, y: 4 (y_hi: 2, y_lo: 2; y = y_hi * 2 + y_lo), z: 4, core: 2. Of those that a mesh axis runs over, the one named last changes fastest.
Arguments:
- hidden_in: bfloat16 [32768, 1280], P(('dp', 'frame')), may hold values from -24 to 24
- rec_lengths: int32 [32, 3], P('dp'), may hold values from 1 to 512, 1024 in all within a row
- token_positions: int32 [32768], P('dp'), may hold values from 0 to 1535, as said below
- thinker_grad: bfloat16 [49152, 1280], P(('dp', 'frame')), may hold values from -6 to 6
- norm_gain: float32 [1280], replicated, may hold values from 0.25 to 1.75
- norm_bias: float32 [1280], replicated, may hold values from -3 to 3
- qkv_weight: bfloat16 [1280, 3, 1280], P('dp', None, 'frame'), may hold values from -10 to 10
Outputs:
- hidden_grad: bfloat16 [32768, 1280], P(('dp', 'frame'))
- weight_grad: float32 [1280, 3, 1280], P('dp', None, 'frame')
The draws below stay inside these ranges and needn't reach their ends.
Inputs may be any that keep to these rules, and one draw needn't show every extreme that they name: `token_positions`: within each block of 1024 entries the positions increase strictly; the first is 0 and the last is 1535.
All inputs are finite; a program needn't handle non-finite values.
Results may differ from the reference program's by a relative error of at most 0.025.
The reference program's roundings to bfloat16 on the way (of `normalized`, `projected`, `out_grad`, `weights_low`, `score_grad` and `proj_grad`) count: a program that leaves them out, or rounds other values in their place, can miss the bound.
Values may be sent and summed in bfloat16 or wider, within the bound.
No kernel may reach another device: no remote copies, remote signals or barrier semaphores. Data moves between devices by JAX's collectives and lax.ppermute only.
A program may use at most 128 MiB of HBM per device.

```python
import math
import jax
import jax.numpy as jnp
import numpy as np
from jax import lax

D = 1280
HEADS = 20
HD = 64
REC = 3
FRAMES_G = 1024
FRAMES = 32768
THINK_G = 1536
THINK_ALL = 49152
MOST = 512
GROUPS = 32


def draw_token_positions(key, part):
    groups = FRAMES // FRAMES_G
    group_keys = jax.random.split(key, groups)

    def one_group(group_key):
        middle = jax.random.permutation(group_key, THINK_G - 2).astype(jnp.int32) + 1
        chosen = jnp.sort(middle[:FRAMES_G - 2])
        return jnp.concatenate([jnp.zeros((1,), jnp.int32), chosen, jnp.full((1,), THINK_G - 1, jnp.int32)])
    return jax.vmap(one_group)(group_keys).reshape(FRAMES)


def draw_qkv_weight(key, part):
    base_key = jax.random.fold_in(jax.random.fold_in(key, 17), 0)
    base = jnp.clip(jax.random.normal(base_key, (D, 3, D), jnp.float32), -4.0, 4.0) * D ** (-0.5)
    return base.astype(jnp.bfloat16)


def with_spikes(drawn, stream_key, source, target, blocks, factor):
    owner, partner = [(jnp.arange(drawn.shape[dim]) // (drawn.shape[dim] // blocks)).reshape([-1 if axis == dim else 1 for axis in range(drawn.ndim)]) for dim in (source, target)]
    chosen = jax.random.permutation(stream_key, blocks)[partner]
    strong = (owner == chosen) | (owner == (partner + blocks // 2) % blocks)
    return jnp.where(strong, factor * drawn, drawn)


def block_levels(own_key, extent, cuts, low, largest):
    def one(axis_at, blocks):
        draws = jax.random.uniform(jax.random.fold_in(jax.random.fold_in(own_key, 6), axis_at), (blocks,), jnp.float32, low / len(cuts), largest / len(cuts))
        return jnp.repeat(jnp.exp(draws), extent[axis_at] // blocks).reshape((-1,) + (1,) * (len(extent) - axis_at - 1))

    level = one(*cuts[0])
    for cut in cuts[1:]:
        level = level * one(*cut)
    return level


def profile(number_of, total, limit, skew):
    weights = [(1 << 20) // math.isqrt(rank ** skew) + 1 for rank in range(2, number_of + 1)]
    rest, given = total - limit - (number_of - 1), [1] * (number_of - 1)
    while rest > 0:
        movable = [i for i in range(number_of - 1) if given[i] < limit]
        mass, budget = sum([weights[i] for i in movable]), rest
        for i in movable:
            more = min(limit - given[i], max(1, budget * weights[i] // mass), rest)
            given[i] = given[i] + more
            rest = rest - more
    return np.array([limit] + given)


def ragged(stream_key, amount, total, limit, skew):
    if amount == 2:
        one = jax.random.randint(stream_key, (), max(1, total - limit), min(limit, total - 1) + 1)
        return jnp.stack([one, total - one])
    tallies = jnp.asarray(profile(amount, total, limit, skew), jnp.int32)
    pairs = (amount - 1) // 2
    donor, sink = tallies[1:1 + 2 * pairs:2], tallies[2:2 + 2 * pairs:2]
    margin = jnp.minimum(donor - 1, limit - sink)
    passed = jax.random.randint(jax.random.fold_in(stream_key, 1), (pairs,), 0, 1 << 20) % (margin + 1)
    tallies = tallies.at[1:1 + 2 * pairs:2].set(donor - passed).at[2:2 + 2 * pairs:2].set(sink + passed)
    return tallies[jax.random.permutation(jax.random.fold_in(stream_key, 2), amount)]


def gaussian(key, dims, spread, limit, shards=(), held_as=jnp.bfloat16):
    entries = spread * jax.random.normal(key, dims, jnp.float32)
    if shards:
        entries = entries * block_levels(key, dims, shards, -0.22, 0.18)
    return jnp.clip(entries, -limit, limit).astype(held_as)


def heavy_noise(rng, dims, scale, most, pieces, heavy, kind=jnp.bfloat16):
    entries = scale * jax.random.normal(rng, dims, jnp.float32)
    if pieces:
        entries = entries * block_levels(rng, dims, pieces, -0.22, 0.18)
    return jnp.clip(with_spikes(entries, jax.random.fold_in(rng, 3), *heavy), -most, most).astype(kind)


def setup_inputs(seed: int = 0) -> dict:
    seeds = jax.random.split(jax.random.key(seed), 8)
    return {
        "hidden_in": heavy_noise(seeds[0], (FRAMES, D), 1.0, 24.0, ((0, 128),), (0, 1, 128, 5.5)),
        "rec_lengths": jax.vmap(lambda own: ragged(own, REC, FRAMES_G, MOST, 2))(jax.random.split(seeds[1], GROUPS)).reshape((GROUPS, REC)).astype(jnp.int32),
        "token_positions": draw_token_positions(jax.random.fold_in(seeds[7], 71), 0),
        "thinker_grad": gaussian(seeds[3], (THINK_ALL, D), 1.0, 6.0, ((0, 128),)),
        "norm_gain": jnp.clip(1.0 + 0.15 * jax.random.normal(seeds[4], (D,), jnp.float32), 0.25, 1.75),
        "norm_bias": gaussian(seeds[5], (D,), 0.5, 3.0, (), jnp.float32),
        "qkv_weight": draw_qkv_weight(jax.random.fold_in(seeds[7], 71), 0),
    }


norm_eps = 1e-05

def norm_forward(rows, gain, bias):
    rows_f32 = rows.astype(jnp.float32)
    mean_row = lax.optimization_barrier(jnp.mean(rows_f32, axis=-1, keepdims=True))
    centered = rows_f32 - mean_row
    variance = lax.optimization_barrier(jnp.mean(centered * centered, axis=-1, keepdims=True))
    inv_std = lax.rsqrt(variance + norm_eps)
    standard = centered * inv_std
    normalized = (standard * gain + bias).astype(jnp.bfloat16)
    return (normalized, standard, inv_std)

def norm_backward(norm_grad, standard, inv_std, gain):
    scaled = norm_grad * gain
    result = inv_std * (scaled - lax.optimization_barrier(jnp.mean(scaled, axis=-1, keepdims=True)) - standard * lax.optimization_barrier(jnp.mean(scaled * standard, axis=-1, keepdims=True)))
    return result.astype(jnp.bfloat16)

def segment_ids(lengths, count):
    ends = jnp.cumsum(lengths.astype(jnp.int32))
    frame_ids = jnp.arange(count, dtype=jnp.int32)
    return lax.optimization_barrier(jnp.sum((frame_ids[:, None] >= ends[None, :]).astype(jnp.int32), axis=1))

def head_backward(queries, keys_in, values, out_grad, segments, score_scale):
    scores = jnp.dot(queries, keys_in.T, preferred_element_type=jnp.float32)
    same_rec = segments[:, None] == segments[None, :]
    scores = jnp.where(same_rec, scores * score_scale, -1e+30)
    row_max = lax.optimization_barrier(jnp.max(scores, axis=-1, keepdims=True))
    expo = jnp.where(same_rec, jnp.exp(scores - row_max), 0.0)
    attn_weights = expo / lax.optimization_barrier(jnp.sum(expo, axis=-1, keepdims=True))
    weight_grads = jnp.dot(out_grad, values.T, preferred_element_type=jnp.float32)
    row_dot = lax.optimization_barrier(jnp.sum(attn_weights * weight_grads, axis=-1, keepdims=True))
    score_grad = (attn_weights * (weight_grads - row_dot)).astype(jnp.bfloat16)
    weights_low = attn_weights.astype(jnp.bfloat16)
    value_grad = jnp.dot(weights_low.T, out_grad, preferred_element_type=jnp.float32)
    query_grad = jnp.dot(score_grad, keys_in, preferred_element_type=jnp.float32) * score_scale
    key_grad = jnp.dot(score_grad.T, queries, preferred_element_type=jnp.float32) * score_scale
    return (query_grad, key_grad, value_grad)

def reference(hidden_in, rec_lengths, token_positions, thinker_grad, norm_gain, norm_bias, qkv_weight):
    groups = FRAMES // FRAMES_G
    score_scale = HD ** (-0.5)
    weight_flat = qkv_weight.reshape(D, 3 * D)
    frames_all = hidden_in.reshape(groups, FRAMES_G, D)
    positions_all = token_positions.reshape(groups, FRAMES_G)
    thinker_all = thinker_grad.reshape(groups, THINK_G, D)

    def group_step(total, items):
        rows, lengths, positions, thinker_rows = items
        normalized, standard, inv_std = norm_forward(rows, norm_gain, norm_bias)
        projected = jnp.dot(normalized, weight_flat, preferred_element_type=jnp.float32)
        projected = projected.astype(jnp.bfloat16).reshape(FRAMES_G, 3, HEADS, HD)
        out_grad = jnp.take(thinker_rows, positions, axis=0).reshape(FRAMES_G, HEADS, HD)
        segments = segment_ids(lengths, FRAMES_G)

        def one_head(head):
            return head_backward(projected[:, 0, head], projected[:, 1, head], projected[:, 2, head], out_grad[:, head], segments, score_scale)
        query_grad, key_grad, value_grad = lax.map(one_head, jnp.arange(HEADS, dtype=jnp.int32))
        stacked = jnp.stack([query_grad, key_grad, value_grad], axis=0)
        proj_grad = jnp.transpose(stacked, (2, 0, 1, 3)).astype(jnp.bfloat16).reshape(FRAMES_G, 3 * D)
        norm_grad = jnp.dot(proj_grad, weight_flat.T, preferred_element_type=jnp.float32)
        weight_part = jnp.dot(normalized.T, proj_grad, preferred_element_type=jnp.float32)
        result = norm_backward(norm_grad, standard, inv_std, norm_gain)
        return (total + weight_part, result)
    start_total = jnp.zeros((D, 3 * D), jnp.float32)
    weight_total, grads = lax.scan(group_step, start_total, (frames_all, rec_lengths, positions_all, thinker_all))
    return (grads.reshape(FRAMES, D).astype(jnp.bfloat16), weight_total.reshape(D, 3, D))
```

```python
import math

import jax
import jax.numpy as jnp
from jax import lax
from jax.sharding import PartitionSpec as P

HD = 64


norm_eps = 1e-05


def norm_forward(rows, gain, bias):
    rows_f32 = rows.astype(jnp.float32)
    mean_row = jnp.mean(rows_f32, axis=-1, keepdims=True)
    centered = rows_f32 - mean_row
    variance = jnp.mean(centered * centered, axis=-1, keepdims=True)
    inv_std = lax.rsqrt(variance + norm_eps)
    standard = centered * inv_std
    normalized = (standard * gain + bias).astype(jnp.bfloat16)
    return (normalized, standard, inv_std)


def norm_backward(norm_grad, standard, inv_std, gain):
    scaled = norm_grad * gain
    result = inv_std * (
        scaled
        - jnp.mean(scaled, axis=-1, keepdims=True)
        - standard * jnp.mean(scaled * standard, axis=-1, keepdims=True)
    )
    return result.astype(jnp.bfloat16)


def segment_ids(lengths, count):
    ends = jnp.cumsum(lengths)
    frame_ids = jnp.arange(count, dtype=jnp.int32)
    return jnp.sum((frame_ids[:, None] >= ends[None, :]).astype(jnp.int32), axis=1)


def head_pass(queries, keys_in, values, out_grad, segments, score_scale, block_rows):
    length = queries.shape[0]
    head_size = queries.shape[1]

    def step(totals, first_row):
        key_total, value_total = totals
        query_rows = lax.dynamic_slice_in_dim(queries, first_row, block_rows, 0)
        grad_rows = lax.dynamic_slice_in_dim(out_grad, first_row, block_rows, 0)
        seg_rows = lax.dynamic_slice_in_dim(segments, first_row, block_rows, 0)
        scores = jnp.einsum("qd,kd->qk", query_rows, keys_in, preferred_element_type=jnp.float32)
        same_rec = seg_rows[:, None] == segments[None, :]
        scores = jnp.where(same_rec, scores * score_scale, -1e30)
        row_max = jnp.max(scores, axis=-1, keepdims=True)
        expo = jnp.where(same_rec, jnp.exp(scores - row_max), 0.0)
        attn_weights = expo / jnp.sum(expo, axis=-1, keepdims=True)
        weight_grads = jnp.einsum(
            "qd,kd->qk", grad_rows, values, preferred_element_type=jnp.float32
        )
        row_dot = jnp.sum(attn_weights * weight_grads, axis=-1, keepdims=True)
        score_grad = (attn_weights * (weight_grads - row_dot)).astype(jnp.bfloat16)
        weights_low = attn_weights.astype(jnp.bfloat16)
        value_total = value_total + jnp.einsum(
            "qk,qd->kd", weights_low, grad_rows, preferred_element_type=jnp.float32
        )
        key_total = key_total + jnp.einsum(
            "qk,qd->kd", score_grad, query_rows, preferred_element_type=jnp.float32
        )
        query_grad = jnp.einsum(
            "qk,kd->qd", score_grad, keys_in, preferred_element_type=jnp.float32
        )
        return ((key_total, value_total), (query_grad * score_scale).astype(jnp.bfloat16))

    starts = jnp.arange(length // block_rows, dtype=jnp.int32) * block_rows
    zero_acc = jnp.zeros((length, head_size), jnp.float32)
    (key_total, value_total), query_grad = lax.scan(step, (zero_acc, zero_acc), starts)
    query_grad = query_grad.reshape(length, head_size)
    return (
        query_grad,
        (key_total * score_scale).astype(jnp.bfloat16),
        value_total.astype(jnp.bfloat16),
    )


def attention_grads(projected, out_grad, segments):
    length = projected.shape[0]
    head_cols = projected.shape[2]
    local_heads = head_cols // HD
    block_rows = math.gcd(length, 512)
    score_scale = HD ** (-0.5)

    def split_heads(block):
        return jnp.transpose(block.reshape(length, local_heads, HD), (1, 0, 2))

    def one_head(items):
        return head_pass(items[0], items[1], items[2], items[3], segments, score_scale, block_rows)

    grads = lax.map(
        one_head,
        (
            split_heads(projected[:, 0]),
            split_heads(projected[:, 1]),
            split_heads(projected[:, 2]),
            split_heads(out_grad),
        ),
    )
    merged = [jnp.transpose(item, (1, 0, 2)).reshape(length, head_cols) for item in grads]
    return jnp.stack(merged, axis=1)


FRAME_SIDE = [(0, 2), (1, 3), (2, 0), (3, 1)]
FRAME_CORE = [(0, 1), (1, 0), (2, 3), (3, 2)]


def gather_frames(rows):
    core = lax.axis_index("frame") % 2
    side = lax.axis_index("frame") // 2
    far = lax.ppermute(rows, "frame", FRAME_SIDE)
    mine = jnp.where(side == 0, jnp.stack([rows, far]), jnp.stack([far, rows]))
    other = lax.ppermute(mine, "frame", FRAME_CORE)
    pair = jnp.where(core == 0, jnp.stack([mine, other], axis=1), jnp.stack([other, mine], axis=1))
    return pair.reshape(4 * rows.shape[0], rows.shape[1])


def scatter_frames(total):
    core = lax.axis_index("frame") % 2
    side = lax.axis_index("frame") // 2
    quarter = total.shape[0] // 4
    blocks = total.reshape(2, 2, quarter, total.shape[1])
    keep = lax.dynamic_index_in_dim(blocks, core, 1, keepdims=False)
    give = lax.dynamic_index_in_dim(blocks, 1 - core, 1, keepdims=False).astype(jnp.bfloat16)
    half = keep + lax.ppermute(give, "frame", FRAME_CORE).astype(jnp.float32)
    keep = lax.dynamic_index_in_dim(half, side, 0, keepdims=False)
    give = lax.dynamic_index_in_dim(half, 1 - side, 0, keepdims=False).astype(jnp.bfloat16)
    return keep + lax.ppermute(give, "frame", FRAME_SIDE).astype(jnp.float32)


def per_device(
    hidden_in, rec_lengths, token_positions, thinker_grad, norm_gain, norm_bias, qkv_weight
):
    frame_count = lax.axis_size("frame")
    groups = lax.axis_size("dp")
    width = hidden_in.shape[1]
    own_rows = qkv_weight.shape[0]
    head_cols = qkv_weight.shape[2]
    group_frames = token_positions.shape[0]
    think_rows = thinker_grad.shape[0]
    flat_weight = qkv_weight.reshape(own_rows, 3 * head_cols)
    weight = lax.all_to_all(
        jnp.broadcast_to(flat_weight[None], (groups, own_rows, 3 * head_cols)), "dp", 0, 0, tiled=True
    ).reshape(width, 3 * head_cols)
    normalized, standard, inv_std = norm_forward(hidden_in, norm_gain, norm_bias)
    normalized = gather_frames(normalized)
    segments = segment_ids(rec_lengths[0], group_frames)
    moved = lax.all_to_all(
        thinker_grad.reshape(think_rows, frame_count, head_cols),
        "frame",
        split_axis=1,
        concat_axis=0,
        tiled=True,
    )
    moved = moved.reshape(frame_count * think_rows, head_cols)
    out_grad = jnp.take(moved, token_positions, axis=0)
    projected = jnp.dot(normalized, weight, preferred_element_type=jnp.float32)
    projected = projected.astype(jnp.bfloat16).reshape(group_frames, 3, head_cols)
    proj_grad = attention_grads(projected, out_grad, segments)
    grad_flat = proj_grad.reshape(group_frames, 3 * head_cols)
    partial = lax.dot_general(
        grad_flat, weight, (((1,), (1,)), ((), ())), preferred_element_type=jnp.float32
    )
    norm_grad = scatter_frames(partial)
    term = lax.dot_general(
        normalized, grad_flat, (((0,), (0,)), ((), ())), preferred_element_type=jnp.float32
    )
    terms = lax.all_to_all(
        term.astype(jnp.bfloat16).reshape(groups, own_rows, 3 * head_cols), "dp", 0, 0, tiled=True
    )
    weight_grad = jnp.sum(terms.astype(jnp.float32), axis=0).reshape(own_rows, 3, head_cols)
    hidden_grad = norm_backward(norm_grad, standard, inv_std, norm_gain)
    return (hidden_grad, weight_grad)


def solution(mesh):
    placed = (
        P(("dp", "frame"), None),
        P("dp", None),
        P("dp"),
        P(("dp", "frame"), None),
        P(),
        P(),
        P("dp", None, "frame"),
    )
    return jax.shard_map(
        per_device,
        mesh=mesh,
        in_specs=placed,
        out_specs=(P(("dp", "frame"), None), P("dp", None, "frame")),
        check_vma=False,
    )
```

```python
import jax
import jax.numpy as jnp
from jax import lax
from jax.experimental import pallas as pl
from jax.experimental.pallas import tpu as pltpu
from jax.sharding import PartitionSpec as P

HD = 64


norm_eps = 1e-05


def norm_forward(rows, gain, bias):
    rows_f32 = rows.astype(jnp.float32)
    mean_row = jnp.mean(rows_f32, axis=-1, keepdims=True)
    centered = rows_f32 - mean_row
    variance = jnp.mean(centered * centered, axis=-1, keepdims=True)
    inv_std = lax.rsqrt(variance + norm_eps)
    standard = centered * inv_std
    normalized = (standard * gain + bias).astype(jnp.bfloat16)
    return (normalized, standard, inv_std)


def norm_backward(norm_grad, standard, inv_std, gain):
    scaled = norm_grad * gain
    result = inv_std * (
        scaled
        - jnp.mean(scaled, axis=-1, keepdims=True)
        - standard * jnp.mean(scaled * standard, axis=-1, keepdims=True)
    )
    return result.astype(jnp.bfloat16)


def segment_ids(lengths, count):
    ends = jnp.cumsum(lengths)
    frame_ids = jnp.arange(count, dtype=jnp.int32)
    return jnp.sum((frame_ids[:, None] >= ends[None, :]).astype(jnp.int32), axis=1)


NEG = -1e30
F32 = jnp.float32
BF16 = jnp.bfloat16
QB = 256
KT = 256

KEY_UPPER = (True, False, True, False, False)
NT = (((1,), (1,)), ((), ()))
TN = (((0,), (0,)), ((), ()))


def attention_kernel(
    bounds, proj_ref, grad_ref, seg_ref, out_ref,
    q_aug, q_pad, k_aug, k_pad, v_pad, g_pad, score, dprob, kv_acc, dq_acc,
):
    rows = proj_ref.shape[0]
    heads = len(KEY_UPPER)
    scale = HD ** (-0.5)
    step_rows = 256

    def prepare(i, carry):
        r = pl.ds(pl.multiple_of(i * step_rows, step_rows), step_rows)
        lane = lax.broadcasted_iota(jnp.int32, (step_rows, 128), 1)
        seg = seg_ref[r, :]
        for h in range(heads):
            upper = KEY_UPPER[h]
            own = (lane >= 64) if upper else (lane < 64)
            slot = lane if upper else lane - 64
            kv = proj_ref[r, 128 * h:128 * (h + 1)].astype(F32)
            if h < 4:
                q = proj_ref[r, 640 + 128 * (h // 2):768 + 128 * (h // 2)].astype(F32)
            else:
                q = jnp.concatenate([proj_ref[r, 896:960].astype(F32), jnp.zeros((step_rows, 64), F32)], axis=1)
            q = q * scale
            g = grad_ref[r, 128 * (h // 2):128 * (h // 2) + 128].astype(F32)
            hit = slot == seg
            q_aug[h, r, :] = jnp.where(own, q, jnp.where(hit, 1.0, 0.0)).astype(BF16)
            q_pad[h, r, :] = jnp.where(own, q, 0.0).astype(BF16)
            miss = jnp.logical_and(jnp.logical_and(slot >= 0, slot < 3), jnp.logical_not(hit))
            k_aug[h, r, :] = jnp.where(own, kv, jnp.where(miss, NEG, 0.0)).astype(BF16)
            k_pad[h, r, :] = jnp.where(own, kv, 0.0).astype(BF16)
            v_pad[h, r, :] = jnp.where(own, 0.0, kv).astype(BF16)
            g_pad[h, r, :] = jnp.where(own, 0.0, g).astype(BF16)
            kv_acc[h, r, :] = jnp.zeros((step_rows, 128), F32)
        return carry

    lax.fori_loop(0, rows // step_rows, prepare, 0)

    def fold(x, op):
        y = x[0:8]
        for i in range(1, x.shape[0] // 8):
            y = op(y, x[8 * i:8 * i + 8])
        return y

    def query_block(qb, carry):
        q0 = pl.multiple_of(qb * QB, QB)
        qr = pl.ds(q0, QB)
        lo, hi = bounds[0, qb], bounds[1, qb]

        def first(t, tops):
            kr = pl.ds(pl.multiple_of(t * KT, KT), KT)
            new = []
            for h in range(heads):
                s = lax.dot_general(k_aug[h, kr, :], q_aug[h, qr, :], NT, preferred_element_type=F32)
                score[h, kr, :] = s
                new.append(jnp.maximum(tops[h], jnp.max(s.reshape(KT // 8, 8, QB), axis=0)))
            return tuple(new)

        tops = lax.fori_loop(lo, hi, first, tuple(jnp.full((8, QB), -3e38, F32) for _ in range(heads)))
        tops = [jnp.max(x, axis=0, keepdims=True) for x in tops]

        def second(t, sums):
            kr = pl.ds(pl.multiple_of(t * KT, KT), KT)
            new = []
            for h in range(heads):
                e = jnp.exp(score[h, kr, :] - tops[h])
                d = lax.dot_general(v_pad[h, kr, :], g_pad[h, qr, :], NT, preferred_element_type=F32)
                score[h, kr, :] = e
                dprob[h, kr, :] = d
                total, dotted = sums[h]
                new.append((
                    total + jnp.sum(e.reshape(KT // 8, 8, QB), axis=0),
                    dotted + jnp.sum((e * d).reshape(KT // 8, 8, QB), axis=0),
                ))
            return tuple(new)

        zero = jnp.zeros((8, QB), F32)
        sums = lax.fori_loop(lo, hi, second, tuple((zero, zero) for _ in range(heads)))
        inv, dot = [], []
        for total, dotted in sums:
            one = 1.0 / jnp.sum(total, axis=0, keepdims=True)
            inv.append(one)
            dot.append(jnp.sum(dotted, axis=0, keepdims=True) * one)
        dq_acc[...] = jnp.zeros(dq_acc.shape, F32)

        def third(t, carry):
            kr = pl.ds(pl.multiple_of(t * KT, KT), KT)
            for h in range(heads):
                a = score[h, kr, :] * inv[h]
                ds = (a * (dprob[h, kr, :] - dot[h])).astype(BF16)
                w = a.astype(BF16)
                kv_acc[h, kr, :] += (
                    jnp.dot(ds, q_pad[h, qr, :], preferred_element_type=F32)
                    + jnp.dot(w, g_pad[h, qr, :], preferred_element_type=F32)
                )
                dq_acc[h // 2] += lax.dot_general(ds, k_pad[h, kr, :], TN, preferred_element_type=F32)
            return carry

        lax.fori_loop(lo, hi, third, 0)
        out_ref[qr, 640:768] = (dq_acc[0] * scale).astype(BF16)
        out_ref[qr, 768:896] = (dq_acc[1] * scale).astype(BF16)
        out_ref[qr, 896:960] = (dq_acc[2] * scale).astype(BF16)[:, :64]
        return carry

    lax.fori_loop(0, rows // QB, query_block, 0)

    def finish(i, carry):
        r = pl.ds(pl.multiple_of(i * step_rows, step_rows), step_rows)
        for h in range(heads):
            out_ref[r, 128 * h:128 * (h + 1)] = kv_acc[h, r, :].astype(BF16)
        return carry

    lax.fori_loop(0, rows // step_rows, finish, 0)


def attention(projected, out_grad, segments, lengths):
    rows = projected.shape[0]
    heads = len(KEY_UPPER)
    ends = jnp.cumsum(lengths)
    starts = ends - lengths
    first_row = jnp.arange(rows // QB, dtype=jnp.int32) * QB
    lo = starts[segments[first_row]] // KT
    hi = (ends[segments[first_row + (QB - 1)]] + KT - 1) // KT
    bounds = jnp.stack([lo, hi]).astype(jnp.int32)
    vm = pl.BlockSpec(memory_space=pltpu.VMEM)
    tall = lambda: pltpu.VMEM((heads, rows, 128), BF16)
    return pl.pallas_call(
        attention_kernel,
        out_shape=jax.ShapeDtypeStruct((rows, projected.shape[1]), BF16),
        in_specs=[pl.BlockSpec(memory_space=pltpu.SMEM), vm, vm, vm],
        out_specs=vm,
        scratch_shapes=[tall() for _ in range(6)] + [
            pltpu.VMEM((heads, rows, QB), F32),
            pltpu.VMEM((heads, rows, QB), F32),
            pltpu.VMEM((heads, rows, 128), F32),
            pltpu.VMEM((3, QB, 128), F32),
        ],
        compiler_params=pltpu.CompilerParams(vmem_limit_bytes=60 << 20),
        cost_estimate=pl.CostEstimate(flops=20_000_000_000, bytes_accessed=6_000_000, transcendentals=5_000_000),
        name="attention_backward",
    )(bounds, projected, out_grad, segments.reshape(rows, 1))


PACK = ((2, 0), (1, 0), (1, 1), (2, 1), (2, 2), (1, 2), (1, 3), (2, 3), (1, 4), (2, 4), (0, 1), (0, 0), (0, 3), (0, 2), (0, 4))


def pack_columns(weight):
    return jnp.concatenate([weight[:, c, HD * h:HD * h + HD] for c, h in PACK], axis=1)


def unpack_columns(packed):
    place = {block: i for i, block in enumerate(PACK)}
    parts = [
        jnp.concatenate([packed[:, HD * place[c, h]:HD * place[c, h] + HD] for h in range(len(KEY_UPPER))], axis=1)
        for c in range(3)
    ]
    return jnp.stack(parts, axis=1)


def grad_tiles(out_grad):
    empty = jnp.zeros((out_grad.shape[0], HD), out_grad.dtype)
    return jnp.concatenate([out_grad[:, :256], empty, out_grad[:, 256:]], axis=1)


FRAME_SIDE = [(0, 2), (1, 3), (2, 0), (3, 1)]
FRAME_CORE = [(0, 1), (1, 0), (2, 3), (3, 2)]


def gather_frames(rows):
    core = lax.axis_index("frame") % 2
    side = lax.axis_index("frame") // 2
    far = lax.ppermute(rows, "frame", FRAME_SIDE)
    mine = jnp.where(side == 0, jnp.stack([rows, far]), jnp.stack([far, rows]))
    other = lax.ppermute(mine, "frame", FRAME_CORE)
    pair = jnp.where(core == 0, jnp.stack([mine, other], axis=1), jnp.stack([other, mine], axis=1))
    return pair.reshape(4 * rows.shape[0], rows.shape[1])


def scatter_frames(total):
    core = lax.axis_index("frame") % 2
    side = lax.axis_index("frame") // 2
    quarter = total.shape[0] // 4
    blocks = total.reshape(2, 2, quarter, total.shape[1])
    keep = lax.dynamic_index_in_dim(blocks, core, 1, keepdims=False)
    give = lax.dynamic_index_in_dim(blocks, 1 - core, 1, keepdims=False).astype(jnp.bfloat16)
    half = keep + lax.ppermute(give, "frame", FRAME_CORE).astype(jnp.float32)
    keep = lax.dynamic_index_in_dim(half, side, 0, keepdims=False)
    give = lax.dynamic_index_in_dim(half, 1 - side, 0, keepdims=False).astype(jnp.bfloat16)
    return keep + lax.ppermute(give, "frame", FRAME_SIDE).astype(jnp.float32)


def per_device(
    hidden_in, rec_lengths, token_positions, thinker_grad, norm_gain, norm_bias, qkv_weight
):
    frame_count = lax.axis_size("frame")
    groups = lax.axis_size("dp")
    width = hidden_in.shape[1]
    own_rows = qkv_weight.shape[0]
    head_cols = qkv_weight.shape[2]
    group_frames = token_positions.shape[0]
    think_rows = thinker_grad.shape[0]
    flat_weight = pack_columns(qkv_weight)
    weight = lax.all_to_all(
        jnp.broadcast_to(flat_weight[None], (groups, own_rows, 3 * head_cols)), "dp", 0, 0, tiled=True
    ).reshape(width, 3 * head_cols)
    normalized, standard, inv_std = norm_forward(hidden_in, norm_gain, norm_bias)
    normalized = gather_frames(normalized)
    segments = segment_ids(rec_lengths[0], group_frames)
    moved = lax.all_to_all(
        thinker_grad.reshape(think_rows, frame_count, head_cols),
        "frame",
        split_axis=1,
        concat_axis=0,
        tiled=True,
    )
    moved = moved.reshape(frame_count * think_rows, head_cols)
    out_grad = jnp.take(moved, token_positions, axis=0)
    projected = jnp.dot(normalized, weight, preferred_element_type=jnp.float32)
    projected = projected.astype(jnp.bfloat16)
    grad_flat = attention(projected, grad_tiles(out_grad), segments, rec_lengths[0])
    partial = lax.dot_general(
        grad_flat, weight, (((1,), (1,)), ((), ())), preferred_element_type=jnp.float32
    )
    norm_grad = scatter_frames(partial)
    term = lax.dot_general(
        normalized, grad_flat, (((0,), (0,)), ((), ())), preferred_element_type=jnp.float32
    )
    terms = lax.all_to_all(
        term.astype(jnp.bfloat16).reshape(groups, own_rows, 3 * head_cols), "dp", 0, 0, tiled=True
    )
    weight_grad = unpack_columns(jnp.sum(terms.astype(jnp.float32), axis=0))
    hidden_grad = norm_backward(norm_grad, standard, inv_std, norm_gain)
    return (hidden_grad, weight_grad)


def solution(mesh):
    placed = (
        P(("dp", "frame"), None),
        P("dp", None),
        P("dp"),
        P(("dp", "frame"), None),
        P(),
        P(),
        P("dp", None, "frame"),
    )
    return jax.shard_map(
        per_device,
        mesh=mesh,
        in_specs=placed,
        out_specs=(P(("dp", "frame"), None), P("dp", None, "frame")),
        check_vma=False,
    )
```

```python
import jax
import jax.numpy as jnp
from jax import lax
from jax.experimental import pallas as pl
from jax.experimental.pallas import tpu as pltpu
from jax.sharding import PartitionSpec as P


HD = 64


norm_eps = 1e-05


def norm_forward(rows, gain, bias):
    rows_f32 = rows.astype(jnp.float32)
    mean_row = jnp.mean(rows_f32, axis=-1, keepdims=True)
    centered = rows_f32 - mean_row
    variance = jnp.mean(centered * centered, axis=-1, keepdims=True)
    inv_std = lax.rsqrt(variance + norm_eps)
    standard = centered * inv_std
    normalized = (standard * gain + bias).astype(jnp.bfloat16)
    return (normalized, standard, inv_std)


def norm_backward(norm_grad, standard, inv_std, gain):
    scaled = norm_grad * gain
    result = inv_std * (
        scaled
        - jnp.mean(scaled, axis=-1, keepdims=True)
        - standard * jnp.mean(scaled * standard, axis=-1, keepdims=True)
    )
    return result.astype(jnp.bfloat16)


def segment_ids(lengths, count):
    ends = jnp.cumsum(lengths)
    frame_ids = jnp.arange(count, dtype=jnp.int32)
    return jnp.sum((frame_ids[:, None] >= ends[None, :]).astype(jnp.int32), axis=1)


NEG = -1e30
F32 = jnp.float32
BF16 = jnp.bfloat16
QB = 256
KT = 256
ROWS = 256

KEY_UPPER = (True, False, True, False, False)
NT = (((1,), (1,)), ((), ()))
TN = (((0,), (0,)), ((), ()))


def chunk_blocks(heads):
    blocks = []
    for h in heads:
        blocks += [(2, h), (1, h)] if KEY_UPPER[h] else [(1, h), (2, h)]
    for h in heads:
        if h % 2 == 0:
            blocks += [(0, h + 1), (0, h)] if h + 1 in heads else [(0, h)]
    return tuple(blocks)


def attention_kernel(
    heads, bounds, norm_ref, weight_ref, grad_ref, seg_ref, out_ref, term_ref,
    q_aug, q_pad, k_aug, k_pad, v_pad, g_pad, score, dprob, kv_acc, dq_acc,
):
    rows = norm_ref.shape[0]
    count = len(heads)
    width = weight_ref.shape[1]
    scale = HD ** (-0.5)

    def prepare(i, carry):
        r = pl.ds(pl.multiple_of(i * ROWS, ROWS), ROWS)
        lane = lax.broadcasted_iota(jnp.int32, (ROWS, 128), 1)
        seg = seg_ref[r, :]
        proj = jnp.dot(norm_ref[r, :], weight_ref[...], preferred_element_type=F32)
        proj = proj.astype(BF16).astype(F32)
        for n, h in enumerate(heads):
            upper = KEY_UPPER[h]
            own = (lane >= 64) if upper else (lane < 64)
            slot = lane if upper else lane - 64
            kv = proj[:, 128 * n:128 * (n + 1)]
            at = 128 * (count + n // 2)
            if at + 128 <= width:
                q = proj[:, at:at + 128]
            else:
                q = jnp.concatenate([proj[:, at:at + 64], jnp.zeros((ROWS, 64), F32)], axis=1)
            q = q * scale
            g = grad_ref[r, 128 * (h // 2):128 * (h // 2) + 128].astype(F32)
            hit = slot == seg
            q_aug[n, r, :] = jnp.where(own, q, jnp.where(hit, 1.0, 0.0)).astype(BF16)
            q_pad[n, r, :] = jnp.where(own, q, 0.0).astype(BF16)
            miss = jnp.logical_and(jnp.logical_and(slot >= 0, slot < 3), jnp.logical_not(hit))
            k_aug[n, r, :] = jnp.where(own, kv, jnp.where(miss, NEG, 0.0)).astype(BF16)
            k_pad[n, r, :] = jnp.where(own, kv, 0.0).astype(BF16)
            v_pad[n, r, :] = jnp.where(own, 0.0, kv).astype(BF16)
            g_pad[n, r, :] = jnp.where(own, 0.0, g).astype(BF16)
            kv_acc[n, r, :] = jnp.zeros((ROWS, 128), F32)
        return carry

    lax.fori_loop(0, rows // ROWS, prepare, 0)

    def query_block(qb, carry):
        qr = pl.ds(pl.multiple_of(qb * QB, QB), QB)
        lo, hi = bounds[0, qb], bounds[1, qb]

        def first(t, tops):
            kr = pl.ds(pl.multiple_of(t * KT, KT), KT)
            new = []
            for h in range(count):
                s = lax.dot_general(k_aug[h, kr, :], q_aug[h, qr, :], NT, preferred_element_type=F32)
                score[h, kr, :] = s
                new.append(jnp.maximum(tops[h], jnp.max(s.reshape(KT // 8, 8, QB), axis=0)))
            return tuple(new)

        tops = lax.fori_loop(lo, hi, first, tuple(jnp.full((8, QB), -3e38, F32) for _ in range(count)))
        tops = [jnp.max(x, axis=0, keepdims=True) for x in tops]

        def second(t, sums):
            kr = pl.ds(pl.multiple_of(t * KT, KT), KT)
            new = []
            for h in range(count):
                e = jnp.exp(score[h, kr, :] - tops[h])
                d = lax.dot_general(v_pad[h, kr, :], g_pad[h, qr, :], NT, preferred_element_type=F32)
                score[h, kr, :] = e
                dprob[h, kr, :] = d
                total, dotted = sums[h]
                new.append((
                    total + jnp.sum(e.reshape(KT // 8, 8, QB), axis=0),
                    dotted + jnp.sum((e * d).reshape(KT // 8, 8, QB), axis=0),
                ))
            return tuple(new)

        zero = jnp.zeros((8, QB), F32)
        sums = lax.fori_loop(lo, hi, second, tuple((zero, zero) for _ in range(count)))
        inv, dot = [], []
        for total, dotted in sums:
            one = 1.0 / jnp.sum(total, axis=0, keepdims=True)
            inv.append(one)
            dot.append(jnp.sum(dotted, axis=0, keepdims=True) * one)
        dq_acc[...] = jnp.zeros(dq_acc.shape, F32)

        def third(t, carry):
            kr = pl.ds(pl.multiple_of(t * KT, KT), KT)
            for h in range(count):
                a = score[h, kr, :] * inv[h]
                ds = (a * (dprob[h, kr, :] - dot[h])).astype(BF16)
                w = a.astype(BF16)
                kv_acc[h, kr, :] += (
                    jnp.dot(ds, q_pad[h, qr, :], preferred_element_type=F32)
                    + jnp.dot(w, g_pad[h, qr, :], preferred_element_type=F32)
                )
                dq_acc[h // 2] += lax.dot_general(ds, k_pad[h, kr, :], TN, preferred_element_type=F32)
            return carry

        lax.fori_loop(lo, hi, third, 0)
        for p in range((count + 1) // 2):
            at = 128 * (count + p)
            span = min(128, width - at)
            out_ref[qr, at:at + span] = (dq_acc[p] * scale).astype(BF16)[:, :span]
        return carry

    lax.fori_loop(0, rows // QB, query_block, 0)

    def finish(i, carry):
        r = pl.ds(pl.multiple_of(i * ROWS, ROWS), ROWS)
        for h in range(count):
            out_ref[r, 128 * h:128 * (h + 1)] = kv_acc[h, r, :].astype(BF16)
        return carry

    lax.fori_loop(0, rows // ROWS, finish, 0)

    for i in range(norm_ref.shape[1] // 256):
        part = lax.dot_general(norm_ref[:, 256 * i:256 * i + 256], out_ref[...], TN, preferred_element_type=F32)
        term_ref[256 * i:256 * i + 256, :] = part.astype(BF16)


def key_bounds(segments, lengths):
    rows = segments.shape[0]
    ends = jnp.cumsum(lengths)
    starts = ends - lengths
    first_row = jnp.arange(rows // QB, dtype=jnp.int32) * QB
    lo = starts[segments[first_row]] // KT
    hi = (ends[segments[first_row + (QB - 1)]] + KT - 1) // KT
    return jnp.stack([lo, hi]).astype(jnp.int32)


def attention(heads, normalized, weight, out_grad, segments, bounds):
    rows, features = normalized.shape
    columns = weight.shape[1]
    count = len(heads)
    vm = pl.BlockSpec(memory_space=pltpu.VMEM)
    tall = pltpu.VMEM((count, rows, 128), BF16)
    wide = pltpu.VMEM((count, rows, QB), F32)
    body = lambda *refs: attention_kernel(heads, *refs)
    return pl.pallas_call(
        body,
        out_shape=(
            jax.ShapeDtypeStruct((rows, columns), BF16),
            jax.ShapeDtypeStruct((features, columns), BF16),
        ),
        in_specs=[pl.BlockSpec(memory_space=pltpu.SMEM), vm, vm, vm, vm],
        out_specs=(vm, vm),
        scratch_shapes=[tall] * 6 + [wide, wide, pltpu.VMEM((count, rows, 128), F32), pltpu.VMEM(((count + 1) // 2, QB, 128), F32)],
        compiler_params=pltpu.CompilerParams(vmem_limit_bytes=40 << 20),
        cost_estimate=pl.CostEstimate(
            flops=5_000_000_000 * count, bytes_accessed=8_000_000, transcendentals=1_000_000 * count
        ),
        name="attention_backward",
    )(bounds, normalized, weight, out_grad, segments)


CHUNKS = ((0, 1), (2, 3, 4))


def pack_columns(weight, heads):
    return jnp.concatenate([weight[:, c, HD * h:HD * h + HD] for c, h in chunk_blocks(heads)], axis=1)


def unpack_columns(chunks):
    place = {}
    for heads, packed in zip(CHUNKS, chunks):
        for i, block in enumerate(chunk_blocks(heads)):
            place[block] = packed[:, HD * i:HD * i + HD]
    parts = [jnp.concatenate([place[c, h] for h in range(len(KEY_UPPER))], axis=1) for c in range(3)]
    return jnp.stack(parts, axis=1)


def gather_weight(shard):
    groups = lax.axis_size("dp")
    spread = lax.all_to_all(jnp.broadcast_to(shard[None], (groups,) + shard.shape), "dp", 0, 0, tiled=True)
    return spread.reshape(groups * shard.shape[0], shard.shape[1])


def exchange_terms(term):
    groups = lax.axis_size("dp")
    return lax.all_to_all(
        term.reshape(groups, term.shape[0] // groups, term.shape[1]), "dp", 0, 0, tiled=True
    )


def grad_tiles(out_grad):
    empty = jnp.zeros((out_grad.shape[0], HD), out_grad.dtype)
    return jnp.concatenate([out_grad[:, :256], empty, out_grad[:, 256:]], axis=1)


FRAME_SIDE = [(0, 2), (1, 3), (2, 0), (3, 1)]
FRAME_CORE = [(0, 1), (1, 0), (2, 3), (3, 2)]


def gather_frames(rows):
    core = lax.axis_index("frame") % 2
    side = lax.axis_index("frame") // 2
    far = lax.ppermute(rows, "frame", FRAME_SIDE)
    mine = jnp.where(side == 0, jnp.stack([rows, far]), jnp.stack([far, rows]))
    other = lax.ppermute(mine, "frame", FRAME_CORE)
    pair = jnp.where(core == 0, jnp.stack([mine, other], axis=1), jnp.stack([other, mine], axis=1))
    return pair.reshape(4 * rows.shape[0], rows.shape[1])


def scatter_frames(total):
    core = lax.axis_index("frame") % 2
    side = lax.axis_index("frame") // 2
    quarter = total.shape[0] // 4
    blocks = total.reshape(2, 2, quarter, total.shape[1])
    keep = lax.dynamic_index_in_dim(blocks, core, 1, keepdims=False)
    give = lax.dynamic_index_in_dim(blocks, 1 - core, 1, keepdims=False).astype(jnp.bfloat16)
    half = keep + lax.ppermute(give, "frame", FRAME_CORE).astype(jnp.float32)
    keep = lax.dynamic_index_in_dim(half, side, 0, keepdims=False)
    give = lax.dynamic_index_in_dim(half, 1 - side, 0, keepdims=False).astype(jnp.bfloat16)
    return keep + lax.ppermute(give, "frame", FRAME_SIDE).astype(jnp.float32)


def per_device(
    hidden_in, rec_lengths, token_positions, thinker_grad, norm_gain, norm_bias, qkv_weight
):
    frame_count = lax.axis_size("frame")
    head_cols = qkv_weight.shape[2]
    group_frames = token_positions.shape[0]
    think_rows = thinker_grad.shape[0]
    shards = [pack_columns(qkv_weight, heads) for heads in CHUNKS]
    normalized, standard, inv_std = norm_forward(hidden_in, norm_gain, norm_bias)
    weights = [gather_weight(shards[0])]
    normalized = gather_frames(normalized)
    thinker, weights[0] = lax.optimization_barrier((thinker_grad, weights[0]))
    moved = lax.all_to_all(
        thinker.reshape(think_rows, frame_count, head_cols),
        "frame",
        split_axis=1,
        concat_axis=0,
        tiled=True,
    )
    shard, moved = lax.optimization_barrier((shards[1], moved))
    weights.append(gather_weight(shard))
    moved = moved.reshape(frame_count * think_rows, head_cols)
    out_grad = grad_tiles(jnp.take(moved, token_positions, axis=0))
    segments = segment_ids(rec_lengths[0], group_frames)
    bounds = key_bounds(segments, rec_lengths[0])
    segments = segments.reshape(group_frames, 1)
    grads, terms = [], []
    for heads, weight in zip(CHUNKS, weights):
        grad, term = attention(heads, normalized, weight, out_grad, segments, bounds)
        grads.append(grad)
        terms.append(exchange_terms(term))
    partial = sum(lax.dot_general(grad, weight, NT, preferred_element_type=F32) for grad, weight in zip(grads, weights))
    norm_grad = scatter_frames(partial)
    weight_grad = unpack_columns([jnp.sum(term.astype(F32), axis=0) for term in terms])
    hidden_grad = norm_backward(norm_grad, standard, inv_std, norm_gain)
    return (hidden_grad, weight_grad)


def solution(mesh):
    placed = (
        P(("dp", "frame"), None),
        P("dp", None),
        P("dp"),
        P(("dp", "frame"), None),
        P(),
        P(),
        P("dp", None, "frame"),
    )

    return jax.shard_map(
        per_device,
        mesh=mesh,
        in_specs=placed,
        out_specs=(P(("dp", "frame"), None), P("dp", None, "frame")),
        check_vma=False,
    )
```

```python
import jax
import jax.numpy as jnp
from jax import lax
from jax.experimental import pallas as pl
from jax.experimental.pallas import tpu as pltpu
from jax.sharding import PartitionSpec as P


HD = 64


norm_eps = 1e-05


def norm_forward(rows, gain, bias):
    rows_f32 = rows.astype(jnp.float32)
    mean_row = jnp.mean(rows_f32, axis=-1, keepdims=True)
    centered = rows_f32 - mean_row
    variance = jnp.mean(centered * centered, axis=-1, keepdims=True)
    inv_std = lax.rsqrt(variance + norm_eps)
    standard = centered * inv_std
    normalized = (standard * gain + bias).astype(jnp.bfloat16)
    return (normalized, standard, inv_std)


def norm_backward(norm_grad, standard, inv_std, gain):
    scaled = norm_grad * gain
    result = inv_std * (
        scaled
        - jnp.mean(scaled, axis=-1, keepdims=True)
        - standard * jnp.mean(scaled * standard, axis=-1, keepdims=True)
    )
    return result.astype(jnp.bfloat16)


NEG = -1e30
F32 = jnp.float32
BF16 = jnp.bfloat16
QB = 256
KT = 256
ROWS = 256

KEY_UPPER = (True, False, True, False, False)
NT = (((1,), (1,)), ((), ()))
TN = (((0,), (0,)), ((), ()))


def chunk_blocks(heads):
    blocks = []
    for h in heads:
        blocks += [(2, h), (1, h)] if KEY_UPPER[h] else [(1, h), (2, h)]
    for h in heads:
        if h % 2 == 0:
            blocks += [(0, h + 1), (0, h)] if h + 1 in heads else [(0, h)]
    return tuple(blocks)


def block_rows(place, j):
    return pl.ds(pl.multiple_of((place ^ j) * ROWS, ROWS), ROWS)


def attention_kernel(
    heads, lengths, place, own, near, far, far_near, weight_ref, grad_ref, out_ref, term_ref,
    norm_ref, q_aug, q_pad, k_aug, k_pad, v_pad, g_pad, score, dprob, kv_acc, dq_acc,
):
    rows = norm_ref.shape[0]
    first_end = lengths[0]
    second_end = first_end + lengths[1]
    for j, piece in enumerate((own, near, far, far_near)):
        norm_ref[block_rows(place[0], j), :] = piece[...]
    count = len(heads)
    width = weight_ref.shape[1]
    scale = HD ** (-0.5)

    def prepare(i, carry):
        r = pl.ds(pl.multiple_of(i * ROWS, ROWS), ROWS)
        lane = lax.broadcasted_iota(jnp.int32, (ROWS, 128), 1)
        frame = i * ROWS + lax.broadcasted_iota(jnp.int32, (ROWS, 128), 0)
        seg = (frame >= first_end).astype(jnp.int32) + (frame >= second_end).astype(jnp.int32)
        proj = jnp.dot(norm_ref[r, :], weight_ref[...], preferred_element_type=F32)
        proj = proj.astype(BF16).astype(F32)
        for n, h in enumerate(heads):
            upper = KEY_UPPER[h]
            own = (lane >= 64) if upper else (lane < 64)
            slot = lane if upper else lane - 64
            kv = proj[:, 128 * n:128 * (n + 1)]
            at = 128 * (count + n // 2)
            if at + 128 <= width:
                q = proj[:, at:at + 128]
            else:
                q = jnp.concatenate([proj[:, at:at + 64], jnp.zeros((ROWS, 64), F32)], axis=1)
            q = q * scale
            g = grad_ref[r, 128 * (h // 2):128 * (h // 2) + 128].astype(F32)
            hit = slot == seg
            q_aug[n, r, :] = jnp.where(own, q, jnp.where(hit, 1.0, 0.0)).astype(BF16)
            q_pad[n, r, :] = jnp.where(own, q, 0.0).astype(BF16)
            miss = jnp.logical_and(jnp.logical_and(slot >= 0, slot < 3), jnp.logical_not(hit))
            k_aug[n, r, :] = jnp.where(own, kv, jnp.where(miss, NEG, 0.0)).astype(BF16)
            k_pad[n, r, :] = jnp.where(own, kv, 0.0).astype(BF16)
            v_pad[n, r, :] = jnp.where(own, 0.0, kv).astype(BF16)
            g_pad[n, r, :] = jnp.where(own, 0.0, g).astype(BF16)
            kv_acc[n, r, :] = jnp.zeros((ROWS, 128), F32)
        return carry

    lax.fori_loop(0, rows // ROWS, prepare, 0)

    def query_block(qb, carry):
        qr = pl.ds(pl.multiple_of(qb * QB, QB), QB)
        head_row, tail_row = qb * QB, qb * QB + (QB - 1)
        start = jnp.where(head_row >= second_end, second_end, jnp.where(head_row >= first_end, first_end, 0))
        end = jnp.where(tail_row >= second_end, rows, jnp.where(tail_row >= first_end, second_end, first_end))
        lo, hi = start // KT, (end + (KT - 1)) // KT

        def first(t, tops):
            kr = pl.ds(pl.multiple_of(t * KT, KT), KT)
            new = []
            for h in range(count):
                s = lax.dot_general(k_aug[h, kr, :], q_aug[h, qr, :], NT, preferred_element_type=F32)
                score[h, kr, :] = s
                new.append(jnp.maximum(tops[h], jnp.max(s.reshape(KT // 8, 8, QB), axis=0)))
            return tuple(new)

        tops = lax.fori_loop(lo, hi, first, tuple(jnp.full((8, QB), -3e38, F32) for _ in range(count)))
        tops = [jnp.max(x, axis=0, keepdims=True) for x in tops]

        def second(t, sums):
            kr = pl.ds(pl.multiple_of(t * KT, KT), KT)
            new = []
            for h in range(count):
                e = jnp.exp(score[h, kr, :] - tops[h])
                d = lax.dot_general(v_pad[h, kr, :], g_pad[h, qr, :], NT, preferred_element_type=F32)
                score[h, kr, :] = e
                dprob[h, kr, :] = d
                total, dotted = sums[h]
                new.append((
                    total + jnp.sum(e.reshape(KT // 8, 8, QB), axis=0),
                    dotted + jnp.sum((e * d).reshape(KT // 8, 8, QB), axis=0),
                ))
            return tuple(new)

        zero = jnp.zeros((8, QB), F32)
        sums = lax.fori_loop(lo, hi, second, tuple((zero, zero) for _ in range(count)))
        inv, dot = [], []
        for total, dotted in sums:
            one = 1.0 / jnp.sum(total, axis=0, keepdims=True)
            inv.append(one)
            dot.append(jnp.sum(dotted, axis=0, keepdims=True) * one)
        dq_acc[...] = jnp.zeros(dq_acc.shape, F32)

        def third(t, carry):
            kr = pl.ds(pl.multiple_of(t * KT, KT), KT)
            for h in range(count):
                a = score[h, kr, :] * inv[h]
                ds = (a * (dprob[h, kr, :] - dot[h])).astype(BF16)
                w = a.astype(BF16)
                kv_acc[h, kr, :] += (
                    jnp.dot(ds, q_pad[h, qr, :], preferred_element_type=F32)
                    + jnp.dot(w, g_pad[h, qr, :], preferred_element_type=F32)
                )
                dq_acc[h // 2] += lax.dot_general(ds, k_pad[h, kr, :], TN, preferred_element_type=F32)
            return carry

        lax.fori_loop(lo, hi, third, 0)
        for p in range((count + 1) // 2):
            at = 128 * (count + p)
            span = min(128, width - at)
            out_ref[qr, at:at + span] = (dq_acc[p] * scale).astype(BF16)[:, :span]
        return carry

    lax.fori_loop(0, rows // QB, query_block, 0)

    def finish(i, carry):
        r = pl.ds(pl.multiple_of(i * ROWS, ROWS), ROWS)
        for h in range(count):
            out_ref[r, 128 * h:128 * (h + 1)] = kv_acc[h, r, :].astype(BF16)
        return carry

    lax.fori_loop(0, rows // ROWS, finish, 0)

    for i in range(norm_ref.shape[1] // 256):
        part = lax.dot_general(norm_ref[:, 256 * i:256 * i + 256], out_ref[...], TN, preferred_element_type=F32)
        term_ref[256 * i:256 * i + 256, :] = part.astype(BF16)


VM = pl.BlockSpec(memory_space=pltpu.VMEM)
SM = pl.BlockSpec(memory_space=pltpu.SMEM)


def attention(heads, lengths, place, pieces, weight, out_grad):
    features, columns = weight.shape
    rows = out_grad.shape[0]
    count = len(heads)
    tall = pltpu.VMEM((count, rows, 128), BF16)
    wide = pltpu.VMEM((count, rows, QB), F32)
    body = lambda *refs: attention_kernel(heads, *refs)
    return pl.pallas_call(
        body,
        out_shape=(
            jax.ShapeDtypeStruct((rows, columns), BF16),
            jax.ShapeDtypeStruct((features, columns), BF16),
        ),
        in_specs=[SM, SM] + [VM] * 6,
        out_specs=(VM, VM),
        scratch_shapes=[pltpu.VMEM((rows, features), BF16)] + [tall] * 6 + [
            wide, wide, pltpu.VMEM((count, rows, 128), F32), pltpu.VMEM(((count + 1) // 2, QB, 128), F32)
        ],
        compiler_params=pltpu.CompilerParams(vmem_limit_bytes=40 << 20),
        cost_estimate=pl.CostEstimate(
            flops=5_000_000_000 * count, bytes_accessed=8_000_000, transcendentals=1_000_000 * count
        ),
        name="attention_backward",
    )(lengths, place, *pieces, weight, out_grad)


def norm_grad_kernel(keep_at, give_at, place, grad_0, grad_1, weight_0, weight_1, keep_ref, give_ref):
    for at, ref in ((give_at, give_ref), (keep_at, keep_ref)):
        r = block_rows(place[0], at)
        total = lax.dot_general(grad_0[r, :], weight_0[...], NT, preferred_element_type=F32)
        total += lax.dot_general(grad_1[r, :], weight_1[...], NT, preferred_element_type=F32)
        ref[...] = total.astype(ref.dtype)


def norm_grad_blocks(keep_at, give_at, place, grads, weights):
    shape = (ROWS, weights[0].shape[0])
    body = lambda *refs: norm_grad_kernel(keep_at, give_at, *refs)
    return pl.pallas_call(
        body,
        out_shape=(jax.ShapeDtypeStruct(shape, F32), jax.ShapeDtypeStruct(shape, BF16)),
        in_specs=[SM] + [VM] * 4,
        out_specs=(VM, VM),
        compiler_params=pltpu.CompilerParams(vmem_limit_bytes=24 << 20),
        cost_estimate=pl.CostEstimate(flops=1_300_000_000, bytes_accessed=6_000_000, transcendentals=0),
        name="norm_grad",
    )(place, *grads, *weights)


CHUNKS = ((0, 1), (2, 3, 4))


def pack_columns(weight, heads):
    return jnp.concatenate([weight[:, c, HD * h:HD * h + HD] for c, h in chunk_blocks(heads)], axis=1)


def unpack_columns(chunks):
    place = {}
    for heads, packed in zip(CHUNKS, chunks):
        for i, block in enumerate(chunk_blocks(heads)):
            place[block] = packed[:, HD * i:HD * i + HD]
    parts = [jnp.concatenate([place[c, h] for h in range(len(KEY_UPPER))], axis=1) for c in range(3)]
    return jnp.stack(parts, axis=1)


def gather_weight(shard):
    groups = lax.axis_size("dp")
    spread = lax.all_to_all(jnp.broadcast_to(shard[None], (groups,) + shard.shape), "dp", 0, 0, tiled=True)
    return spread.reshape(groups * shard.shape[0], shard.shape[1])


def exchange_terms(term):
    groups = lax.axis_size("dp")
    return lax.all_to_all(
        term.reshape(groups, term.shape[0] // groups, term.shape[1]), "dp", 0, 0, tiled=True
    )


def grad_tiles(out_grad):
    empty = jnp.zeros((out_grad.shape[0], HD), out_grad.dtype)
    return jnp.concatenate([out_grad[:, :256], empty, out_grad[:, 256:]], axis=1)


FRAME_SIDE = [(0, 2), (1, 3), (2, 0), (3, 1)]
FRAME_CORE = [(0, 1), (1, 0), (2, 3), (3, 2)]


def swap_side(block):
    return lax.ppermute(block, "frame", FRAME_SIDE)


def swap_core(block):
    return lax.ppermute(block, "frame", FRAME_CORE)


def per_device(
    hidden_in, rec_lengths, token_positions, thinker_grad, norm_gain, norm_bias, qkv_weight
):
    head_cols = qkv_weight.shape[2]
    think_rows = thinker_grad.shape[0]
    place = lax.axis_index("frame")
    side, core = place // 2, place % 2
    shards = [pack_columns(qkv_weight, heads) for heads in CHUNKS]
    weights = [gather_weight(shards[0])]
    own, standard, inv_std = norm_forward(hidden_in, norm_gain, norm_bias)
    far = swap_side(own)
    near = swap_core(own)
    sides = [lax.dynamic_slice_in_dim(thinker_grad, 2 * head_cols * at, 2 * head_cols, 1) for at in (side, 1 - side)]
    far_think = swap_side(sides[1])
    cols = lambda block, at: lax.dynamic_slice_in_dim(block, head_cols * at, head_cols, 1)
    near_think = swap_core(cols(sides[0], 1 - core))
    far_near = swap_core(far)
    far_near_think = swap_core(cols(far_think, 1 - core))
    shard, weights[0] = lax.optimization_barrier((shards[1], weights[0]))
    weights.append(gather_weight(shard))
    moved = jnp.concatenate([cols(sides[0], core), near_think, cols(far_think, core), far_near_think], axis=0)
    rows_at = ((token_positions // think_rows) ^ place) * think_rows + token_positions % think_rows
    out_grad = grad_tiles(jnp.take(moved, rows_at, axis=0))
    pieces = (own, near, far, far_near)
    at = place.reshape(1)
    grads, terms = [], []
    for heads, weight in zip(CHUNKS, weights):
        grad, term = attention(heads, rec_lengths[0], at, pieces, weight, out_grad)
        grads.append(grad)
        terms.append(exchange_terms(term))
    keep, give = norm_grad_blocks(2, 3, at, grads, weights)
    got = swap_core(give)
    side_sum = swap_side((keep + got.astype(F32)).astype(BF16))
    keep, give = norm_grad_blocks(0, 1, at, grads, weights)
    core_sum = swap_core(give)
    norm_grad = keep + core_sum.astype(F32) + side_sum.astype(F32)
    weight_grad = unpack_columns([jnp.sum(term.astype(F32), axis=0) for term in terms])
    hidden_grad = norm_backward(norm_grad, standard, inv_std, norm_gain)
    return (hidden_grad, weight_grad)


def solution(mesh):
    placed = (
        P(("dp", "frame"), None),
        P("dp", None),
        P("dp"),
        P(("dp", "frame"), None),
        P(),
        P(),
        P("dp", None, "frame"),
    )

    return jax.shard_map(
        per_device,
        mesh=mesh,
        in_specs=placed,
        out_specs=(P(("dp", "frame"), None), P("dp", None, "frame")),
        check_vma=False,
    )
```

```python
import jax
import jax.numpy as jnp
from jax import lax
from jax.experimental import pallas as pl
from jax.experimental.pallas import tpu as pltpu
from jax.sharding import PartitionSpec as P


HD = 64


norm_eps = 1e-05


def norm_forward(rows, gain, bias):
    rows_f32 = rows.astype(jnp.float32)
    mean_row = jnp.mean(rows_f32, axis=-1, keepdims=True)
    centered = rows_f32 - mean_row
    variance = jnp.mean(centered * centered, axis=-1, keepdims=True)
    inv_std = lax.rsqrt(variance + norm_eps)
    standard = centered * inv_std
    normalized = (standard * gain + bias).astype(jnp.bfloat16)
    return (normalized, standard, inv_std)


def norm_backward(norm_grad, standard, inv_std, gain):
    scaled = norm_grad * gain
    result = inv_std * (
        scaled
        - jnp.mean(scaled, axis=-1, keepdims=True)
        - standard * jnp.mean(scaled * standard, axis=-1, keepdims=True)
    )
    return result.astype(jnp.bfloat16)


NEG = -1e30
F32 = jnp.float32
BF16 = jnp.bfloat16
QB = 256
KT = 256
ROWS = 256

KEY_UPPER = (True, False, True, False, False)
NT = (((1,), (1,)), ((), ()))
TN = (((0,), (0,)), ((), ()))


def chunk_blocks(heads):
    blocks = []
    for h in heads:
        blocks += [(2, h), (1, h)] if KEY_UPPER[h] else [(1, h), (2, h)]
    for h in heads:
        if h % 2 == 0:
            blocks += [(0, h + 1), (0, h)] if h + 1 in heads else [(0, h)]
    return tuple(blocks)


def block_rows(place, j):
    return pl.ds(pl.multiple_of((place ^ j) * ROWS, ROWS), ROWS)


def attention_kernel(
    heads, lengths, place, own, near, far, far_near, weight_ref, grad_ref, out_ref, term_ref,
    norm_ref, q_aug, q_pad, k_aug, k_pad, v_pad, g_pad, score, dprob, kv_acc, dq_acc,
):
    rows = norm_ref.shape[0]
    first_end = lengths[0]
    second_end = first_end + lengths[1]
    for j, piece in enumerate((own, near, far, far_near)):
        norm_ref[block_rows(place[0], j), :] = piece[...]
    count = len(heads)
    width = weight_ref.shape[1]
    scale = HD ** (-0.5)

    def prepare(i, carry):
        r = pl.ds(pl.multiple_of(i * ROWS, ROWS), ROWS)
        lane = lax.broadcasted_iota(jnp.int32, (ROWS, 128), 1)
        frame = i * ROWS + lax.broadcasted_iota(jnp.int32, (ROWS, 128), 0)
        seg = (frame >= first_end).astype(jnp.int32) + (frame >= second_end).astype(jnp.int32)
        proj = jnp.dot(norm_ref[r, :], weight_ref[...], preferred_element_type=F32)
        proj = proj.astype(BF16).astype(F32)
        for n, h in enumerate(heads):
            upper = KEY_UPPER[h]
            own = (lane >= 64) if upper else (lane < 64)
            slot = lane if upper else lane - 64
            kv = proj[:, 128 * n:128 * (n + 1)]
            at = 128 * (count + n // 2)
            if at + 128 <= width:
                q = proj[:, at:at + 128]
            else:
                q = jnp.concatenate([proj[:, at:at + 64], jnp.zeros((ROWS, 64), F32)], axis=1)
            q = q * scale
            g = grad_ref[r, 128 * (h // 2):128 * (h // 2) + 128].astype(F32)
            hit = slot == seg
            q_aug[n, r, :] = jnp.where(own, q, jnp.where(hit, 1.0, 0.0)).astype(BF16)
            q_pad[n, r, :] = jnp.where(own, q, 0.0).astype(BF16)
            miss = jnp.logical_and(jnp.logical_and(slot >= 0, slot < 3), jnp.logical_not(hit))
            k_aug[n, r, :] = jnp.where(own, kv, jnp.where(miss, NEG, 0.0)).astype(BF16)
            k_pad[n, r, :] = jnp.where(own, kv, 0.0).astype(BF16)
            v_pad[n, r, :] = jnp.where(own, 0.0, kv).astype(BF16)
            g_pad[n, r, :] = jnp.where(own, 0.0, g).astype(BF16)
            kv_acc[n, r, :] = jnp.zeros((ROWS, 128), F32)
        return carry

    lax.fori_loop(0, rows // ROWS, prepare, 0)

    def query_block(qb, carry):
        qr = pl.ds(pl.multiple_of(qb * QB, QB), QB)
        head_row, tail_row = qb * QB, qb * QB + (QB - 1)
        start = jnp.where(head_row >= second_end, second_end, jnp.where(head_row >= first_end, first_end, 0))
        end = jnp.where(tail_row >= second_end, rows, jnp.where(tail_row >= first_end, second_end, first_end))
        lo, hi = start // KT, (end + (KT - 1)) // KT

        def first(t, tops):
            kr = pl.ds(pl.multiple_of(t * KT, KT), KT)
            new = []
            for h in range(count):
                s = lax.dot_general(k_aug[h, kr, :], q_aug[h, qr, :], NT, preferred_element_type=F32)
                score[h, kr, :] = s
                new.append(jnp.maximum(tops[h], jnp.max(s.reshape(KT // 8, 8, QB), axis=0)))
            return tuple(new)

        tops = lax.fori_loop(lo, hi, first, tuple(jnp.full((8, QB), -3e38, F32) for _ in range(count)))
        tops = [jnp.max(x, axis=0, keepdims=True) for x in tops]

        def second(t, sums):
            kr = pl.ds(pl.multiple_of(t * KT, KT), KT)
            new = []
            for h in range(count):
                e = jnp.exp(score[h, kr, :] - tops[h])
                d = lax.dot_general(v_pad[h, kr, :], g_pad[h, qr, :], NT, preferred_element_type=F32)
                score[h, kr, :] = e
                dprob[h, kr, :] = d
                total, dotted = sums[h]
                new.append((
                    total + jnp.sum(e.reshape(KT // 8, 8, QB), axis=0),
                    dotted + jnp.sum((e * d).reshape(KT // 8, 8, QB), axis=0),
                ))
            return tuple(new)

        zero = jnp.zeros((8, QB), F32)
        sums = lax.fori_loop(lo, hi, second, tuple((zero, zero) for _ in range(count)))
        inv, dot = [], []
        for total, dotted in sums:
            one = 1.0 / jnp.sum(total, axis=0, keepdims=True)
            inv.append(one)
            dot.append(jnp.sum(dotted, axis=0, keepdims=True) * one)
        dq_acc[...] = jnp.zeros(dq_acc.shape, F32)

        def third(t, carry):
            kr = pl.ds(pl.multiple_of(t * KT, KT), KT)
            for h in range(count):
                a = score[h, kr, :] * inv[h]
                ds = (a * (dprob[h, kr, :] - dot[h])).astype(BF16)
                w = a.astype(BF16)
                kv_acc[h, kr, :] += (
                    jnp.dot(ds, q_pad[h, qr, :], preferred_element_type=F32)
                    + jnp.dot(w, g_pad[h, qr, :], preferred_element_type=F32)
                )
                dq_acc[h // 2] += lax.dot_general(ds, k_pad[h, kr, :], TN, preferred_element_type=F32)
            return carry

        lax.fori_loop(lo, hi, third, 0)
        for p in range((count + 1) // 2):
            at = 128 * (count + p)
            span = min(128, width - at)
            out_ref[qr, at:at + span] = (dq_acc[p] * scale).astype(BF16)[:, :span]
        return carry

    lax.fori_loop(0, rows // QB, query_block, 0)

    def finish(i, carry):
        r = pl.ds(pl.multiple_of(i * ROWS, ROWS), ROWS)
        for h in range(count):
            out_ref[r, 128 * h:128 * (h + 1)] = kv_acc[h, r, :].astype(BF16)
        return carry

    lax.fori_loop(0, rows // ROWS, finish, 0)

    for i in range(norm_ref.shape[1] // 256):
        part = lax.dot_general(norm_ref[:, 256 * i:256 * i + 256], out_ref[...], TN, preferred_element_type=F32)
        term_ref[256 * i:256 * i + 256, :] = part.astype(BF16)


VM = pl.BlockSpec(memory_space=pltpu.VMEM)
SM = pl.BlockSpec(memory_space=pltpu.SMEM)


def attention(heads, lengths, place, pieces, weight, out_grad):
    features, columns = weight.shape
    rows = out_grad.shape[0]
    count = len(heads)
    tall = pltpu.VMEM((count, rows, 128), BF16)
    wide = pltpu.VMEM((count, rows, QB), F32)
    body = lambda *refs: attention_kernel(heads, *refs)
    return pl.pallas_call(
        body,
        out_shape=(
            jax.ShapeDtypeStruct((rows, columns), BF16),
            jax.ShapeDtypeStruct((features, columns), BF16),
        ),
        in_specs=[SM, SM] + [VM] * 6,
        out_specs=(VM, VM),
        scratch_shapes=[pltpu.VMEM((rows, features), BF16)] + [tall] * 6 + [
            wide, wide, pltpu.VMEM((count, rows, 128), F32), pltpu.VMEM(((count + 1) // 2, QB, 128), F32)
        ],
        compiler_params=pltpu.CompilerParams(vmem_limit_bytes=40 << 20),
        cost_estimate=pl.CostEstimate(
            flops=5_000_000_000 * count, bytes_accessed=8_000_000, transcendentals=1_000_000 * count
        ),
        name="attention_backward",
    )(lengths, place, *pieces, weight, out_grad)


def norm_grad_kernel(keep_at, give_at, place, grad_0, grad_1, weight_0, weight_1, keep_ref, give_ref):
    for at, ref in ((give_at, give_ref), (keep_at, keep_ref)):
        r = block_rows(place[0], at)
        total = lax.dot_general(grad_0[r, :], weight_0[...], NT, preferred_element_type=F32)
        total += lax.dot_general(grad_1[r, :], weight_1[...], NT, preferred_element_type=F32)
        ref[...] = total.astype(ref.dtype)


def norm_grad_blocks(keep_at, give_at, place, grads, weights):
    shape = (ROWS, weights[0].shape[0])
    body = lambda *refs: norm_grad_kernel(keep_at, give_at, *refs)
    return pl.pallas_call(
        body,
        out_shape=(jax.ShapeDtypeStruct(shape, F32), jax.ShapeDtypeStruct(shape, BF16)),
        in_specs=[SM] + [VM] * 4,
        out_specs=(VM, VM),
        compiler_params=pltpu.CompilerParams(vmem_limit_bytes=24 << 20),
        cost_estimate=pl.CostEstimate(flops=1_300_000_000, bytes_accessed=6_000_000, transcendentals=0),
        name="norm_grad",
    )(place, *grads, *weights)


CHUNKS = ((0, 1), (2, 3, 4))


def pack_columns(weight, heads):
    return jnp.concatenate([weight[:, c, HD * h:HD * h + HD] for c, h in chunk_blocks(heads)], axis=1)


def unpack_columns(chunks):
    place = {}
    for heads, packed in zip(CHUNKS, chunks):
        for i, block in enumerate(chunk_blocks(heads)):
            place[block] = packed[:, HD * i:HD * i + HD]
    parts = [jnp.concatenate([place[c, h] for h in range(len(KEY_UPPER))], axis=1) for c in range(3)]
    return jnp.stack(parts, axis=1)


def plane_groups(groups):
    return [list(range(first, groups, 2)) for first in range(2)]


def swap_pair(block):
    groups = lax.axis_size("dp")
    return lax.ppermute(block, "dp", [(i, i ^ 1) for i in range(groups)])


def gather_plane(block):
    groups = lax.axis_size("dp")
    spread = lax.all_to_all(
        jnp.broadcast_to(block[None], (groups // 2,) + block.shape), "dp", 0, 0,
        axis_index_groups=plane_groups(groups), tiled=True,
    )
    return spread.reshape(groups // 2 * block.shape[0], block.shape[1])


def exchange_terms(term):
    groups = lax.axis_size("dp")
    return lax.all_to_all(
        term.reshape(groups // 2, term.shape[0] * 2 // groups, term.shape[1]), "dp", 0, 0,
        axis_index_groups=plane_groups(groups), tiled=True,
    )


def sum_terms(terms):
    second = lax.axis_index("dp") % 2
    total = jnp.sum(terms.astype(F32), axis=0)
    halves = total.reshape(2, total.shape[0] // 2, total.shape[1])
    keep = lax.dynamic_index_in_dim(halves, second, 0, keepdims=False)
    give = lax.dynamic_index_in_dim(halves, 1 - second, 0, keepdims=False)
    return keep + swap_pair(give.astype(BF16)).astype(F32)


def grad_tiles(out_grad):
    empty = jnp.zeros((out_grad.shape[0], HD), out_grad.dtype)
    return jnp.concatenate([out_grad[:, :256], empty, out_grad[:, 256:]], axis=1)


FRAME_SIDE = [(0, 2), (1, 3), (2, 0), (3, 1)]
FRAME_CORE = [(0, 1), (1, 0), (2, 3), (3, 2)]


def swap_side(block):
    return lax.ppermute(block, "frame", FRAME_SIDE)


def swap_core(block):
    return lax.ppermute(block, "frame", FRAME_CORE)


def per_device(
    hidden_in, rec_lengths, token_positions, thinker_grad, norm_gain, norm_bias, qkv_weight
):
    head_cols = qkv_weight.shape[2]
    think_rows = thinker_grad.shape[0]
    place = lax.axis_index("frame")
    side, core = place // 2, place % 2
    shard = jnp.concatenate([pack_columns(qkv_weight, heads) for heads in CHUNKS], axis=1)
    other = swap_pair(shard)
    both = jnp.where(lax.axis_index("dp") % 2 == 0, jnp.concatenate([shard, other]), jnp.concatenate([other, shard]))
    cut = HD * len(chunk_blocks(CHUNKS[0]))
    shards = [both[:, :cut], both[:, cut:]]
    weights = [gather_plane(shards[0])]
    own, standard, inv_std = norm_forward(hidden_in, norm_gain, norm_bias)
    far = swap_side(own)
    near = swap_core(own)
    sides = [lax.dynamic_slice_in_dim(thinker_grad, 2 * head_cols * at, 2 * head_cols, 1) for at in (side, 1 - side)]
    far_think = swap_side(sides[1])
    cols = lambda block, at: lax.dynamic_slice_in_dim(block, head_cols * at, head_cols, 1)
    near_think = swap_core(cols(sides[0], 1 - core))
    far_near = swap_core(far)
    far_near_think = swap_core(cols(far_think, 1 - core))
    shard, weights[0] = lax.optimization_barrier((shards[1], weights[0]))
    weights.append(gather_plane(shard))
    moved = jnp.concatenate([cols(sides[0], core), near_think, cols(far_think, core), far_near_think], axis=0)
    rows_at = ((token_positions // think_rows) ^ place) * think_rows + token_positions % think_rows
    out_grad = grad_tiles(jnp.take(moved, rows_at, axis=0))
    pieces = (own, near, far, far_near)
    at = place.reshape(1)
    grads, terms = [], []
    for heads, weight in zip(CHUNKS, weights):
        grad, term = attention(heads, rec_lengths[0], at, pieces, weight, out_grad)
        grads.append(grad)
        terms.append(exchange_terms(term))
    keep, give = norm_grad_blocks(2, 3, at, grads, weights)
    got = swap_core(give)
    side_sum = swap_side((keep + got.astype(F32)).astype(BF16))
    keep, give = norm_grad_blocks(0, 1, at, grads, weights)
    core_sum = swap_core(give)
    norm_grad = keep + core_sum.astype(F32) + side_sum.astype(F32)
    weight_grad = unpack_columns([sum_terms(term) for term in terms])
    hidden_grad = norm_backward(norm_grad, standard, inv_std, norm_gain)
    return (hidden_grad, weight_grad)


def solution(mesh):
    placed = (
        P(("dp", "frame"), None),
        P("dp", None),
        P("dp"),
        P(("dp", "frame"), None),
        P(),
        P(),
        P("dp", None, "frame"),
    )

    return jax.shard_map(
        per_device,
        mesh=mesh,
        in_specs=placed,
        out_specs=(P(("dp", "frame"), None), P("dp", None, "frame")),
        check_vma=False,
    )
```

```python
import jax
import jax.numpy as jnp
from jax import lax
from jax.experimental import pallas as pl
from jax.experimental.pallas import tpu as pltpu
from jax.sharding import PartitionSpec as P


HD = 64


norm_eps = 1e-05


def norm_forward(rows, gain, bias):
    rows_f32 = rows.astype(jnp.float32)
    mean_row = jnp.mean(rows_f32, axis=-1, keepdims=True)
    centered = rows_f32 - mean_row
    variance = jnp.mean(centered * centered, axis=-1, keepdims=True)
    inv_std = lax.rsqrt(variance + norm_eps)
    standard = centered * inv_std
    normalized = (standard * gain + bias).astype(jnp.bfloat16)
    return (normalized, standard, inv_std)


def norm_backward(norm_grad, standard, inv_std, gain):
    scaled = norm_grad * gain
    result = inv_std * (
        scaled
        - jnp.mean(scaled, axis=-1, keepdims=True)
        - standard * jnp.mean(scaled * standard, axis=-1, keepdims=True)
    )
    return result.astype(jnp.bfloat16)


NEG = -1e30
F32 = jnp.float32
BF16 = jnp.bfloat16
QB = 256
KT = 256
ROWS = 256

KEY_UPPER = (True, False, True, False, False)
NT = (((1,), (1,)), ((), ()))
TN = (((0,), (0,)), ((), ()))


def chunk_blocks(heads):
    blocks = []
    for h in heads:
        blocks += [(2, h), (1, h)] if KEY_UPPER[h] else [(1, h), (2, h)]
    for h in heads:
        if h % 2 == 0:
            blocks += [(0, h + 1), (0, h)] if h + 1 in heads else [(0, h)]
    return tuple(blocks)


def block_rows(place, j):
    return pl.ds(pl.multiple_of((place ^ j) * ROWS, ROWS), ROWS)


def attention_kernel(
    heads, lengths, place, own, near, far, far_near, weight_ref, grad_ref, out_ref, term_ref,
    norm_ref, q_aug, q_pad, k_aug, k_pad, v_pad, g_pad, score, dprob, kv_acc, dq_acc,
):
    rows = norm_ref.shape[0]
    first_end = lengths[0]
    second_end = first_end + lengths[1]
    for j, piece in enumerate((own, near, far, far_near)):
        norm_ref[block_rows(place[0], j), :] = piece[...]
    count = len(heads)
    width = weight_ref.shape[1]
    scale = HD ** (-0.5)

    def prepare(i, carry):
        r = pl.ds(pl.multiple_of(i * ROWS, ROWS), ROWS)
        lane = lax.broadcasted_iota(jnp.int32, (ROWS, 128), 1)
        frame = i * ROWS + lax.broadcasted_iota(jnp.int32, (ROWS, 128), 0)
        seg = (frame >= first_end).astype(jnp.int32) + (frame >= second_end).astype(jnp.int32)
        proj = jnp.dot(norm_ref[r, :], weight_ref[...], preferred_element_type=F32)
        proj = proj.astype(BF16).astype(F32)
        for n, h in enumerate(heads):
            upper = KEY_UPPER[h]
            own = (lane >= 64) if upper else (lane < 64)
            slot = lane if upper else lane - 64
            kv = proj[:, 128 * n:128 * (n + 1)]
            at = 128 * (count + n // 2)
            if at + 128 <= width:
                q = proj[:, at:at + 128]
            else:
                q = jnp.concatenate([proj[:, at:at + 64], jnp.zeros((ROWS, 64), F32)], axis=1)
            q = q * scale
            g = grad_ref[r, 128 * (h // 2):128 * (h // 2) + 128].astype(F32)
            hit = slot == seg
            q_aug[n, r, :] = jnp.where(own, q, jnp.where(hit, 1.0, 0.0)).astype(BF16)
            q_pad[n, r, :] = jnp.where(own, q, 0.0).astype(BF16)
            miss = jnp.logical_and(jnp.logical_and(slot >= 0, slot < 3), jnp.logical_not(hit))
            k_aug[n, r, :] = jnp.where(own, kv, jnp.where(miss, NEG, 0.0)).astype(BF16)
            k_pad[n, r, :] = jnp.where(own, kv, 0.0).astype(BF16)
            v_pad[n, r, :] = jnp.where(own, 0.0, kv).astype(BF16)
            g_pad[n, r, :] = jnp.where(own, 0.0, g).astype(BF16)
            kv_acc[n, r, :] = jnp.zeros((ROWS, 128), F32)
        return carry

    lax.fori_loop(0, rows // ROWS, prepare, 0)

    def query_block(qb, carry):
        qr = pl.ds(pl.multiple_of(qb * QB, QB), QB)
        head_row, tail_row = qb * QB, qb * QB + (QB - 1)
        start = jnp.where(head_row >= second_end, second_end, jnp.where(head_row >= first_end, first_end, 0))
        end = jnp.where(tail_row >= second_end, rows, jnp.where(tail_row >= first_end, second_end, first_end))
        lo, hi = start // KT, (end + (KT - 1)) // KT

        def first(t, tops):
            kr = pl.ds(pl.multiple_of(t * KT, KT), KT)
            new = []
            for h in range(count):
                s = lax.dot_general(k_aug[h, kr, :], q_aug[h, qr, :], NT, preferred_element_type=F32)
                score[h, kr, :] = s
                new.append(jnp.maximum(tops[h], jnp.max(s.reshape(KT // 8, 8, QB), axis=0)))
            return tuple(new)

        tops = lax.fori_loop(lo, hi, first, tuple(jnp.full((8, QB), -3e38, F32) for _ in range(count)))
        tops = [jnp.max(x, axis=0, keepdims=True) for x in tops]

        def second(t, sums):
            kr = pl.ds(pl.multiple_of(t * KT, KT), KT)
            new = []
            for h in range(count):
                e = jnp.exp(score[h, kr, :] - tops[h])
                d = lax.dot_general(v_pad[h, kr, :], g_pad[h, qr, :], NT, preferred_element_type=F32)
                score[h, kr, :] = e
                dprob[h, kr, :] = d
                total, dotted = sums[h]
                new.append((
                    total + jnp.sum(e.reshape(KT // 8, 8, QB), axis=0),
                    dotted + jnp.sum((e * d).reshape(KT // 8, 8, QB), axis=0),
                ))
            return tuple(new)

        zero = jnp.zeros((8, QB), F32)
        sums = lax.fori_loop(lo, hi, second, tuple((zero, zero) for _ in range(count)))
        inv, dot = [], []
        for total, dotted in sums:
            one = 1.0 / jnp.sum(total, axis=0, keepdims=True)
            inv.append(one)
            dot.append(jnp.sum(dotted, axis=0, keepdims=True) * one)
        dq_acc[...] = jnp.zeros(dq_acc.shape, F32)

        def third(t, carry):
            kr = pl.ds(pl.multiple_of(t * KT, KT), KT)
            for h in range(count):
                a = score[h, kr, :] * inv[h]
                ds = (a * (dprob[h, kr, :] - dot[h])).astype(BF16)
                w = a.astype(BF16)
                kv_acc[h, kr, :] += (
                    jnp.dot(ds, q_pad[h, qr, :], preferred_element_type=F32)
                    + jnp.dot(w, g_pad[h, qr, :], preferred_element_type=F32)
                )
                dq_acc[h // 2] += lax.dot_general(ds, k_pad[h, kr, :], TN, preferred_element_type=F32)
            return carry

        lax.fori_loop(lo, hi, third, 0)
        for p in range((count + 1) // 2):
            at = 128 * (count + p)
            span = min(128, width - at)
            out_ref[qr, at:at + span] = (dq_acc[p] * scale).astype(BF16)[:, :span]
        return carry

    lax.fori_loop(0, rows // QB, query_block, 0)

    def finish(i, carry):
        r = pl.ds(pl.multiple_of(i * ROWS, ROWS), ROWS)
        for h in range(count):
            out_ref[r, 128 * h:128 * (h + 1)] = kv_acc[h, r, :].astype(BF16)
        return carry

    lax.fori_loop(0, rows // ROWS, finish, 0)

    for i in range(norm_ref.shape[1] // 256):
        part = lax.dot_general(norm_ref[:, 256 * i:256 * i + 256], out_ref[...], TN, preferred_element_type=F32)
        term_ref[256 * i:256 * i + 256, :] = part.astype(BF16)


VM = pl.BlockSpec(memory_space=pltpu.VMEM)
SM = pl.BlockSpec(memory_space=pltpu.SMEM)


def attention(heads, lengths, place, pieces, weight, out_grad):
    features, columns = weight.shape
    rows = out_grad.shape[0]
    count = len(heads)
    tall = pltpu.VMEM((count, rows, 128), BF16)
    wide = pltpu.VMEM((count, rows, QB), F32)
    body = lambda *refs: attention_kernel(heads, *refs)
    return pl.pallas_call(
        body,
        out_shape=(
            jax.ShapeDtypeStruct((rows, columns), BF16),
            jax.ShapeDtypeStruct((features, columns), BF16),
        ),
        in_specs=[SM, SM] + [VM] * 6,
        out_specs=(VM, VM),
        scratch_shapes=[pltpu.VMEM((rows, features), BF16)] + [tall] * 6 + [
            wide, wide, pltpu.VMEM((count, rows, 128), F32), pltpu.VMEM(((count + 1) // 2, QB, 128), F32)
        ],
        compiler_params=pltpu.CompilerParams(vmem_limit_bytes=(12 + 5 * count) << 20),
        cost_estimate=pl.CostEstimate(
            flops=5_000_000_000 * count, bytes_accessed=8_000_000, transcendentals=1_000_000 * count
        ),
        name="attention_backward",
    )(lengths, place, *pieces, weight, out_grad)


def norm_grad_kernel(keep_at, give_at, place, grad_0, grad_1, weight_0, weight_1, keep_ref, give_ref):
    for at, ref in ((give_at, give_ref), (keep_at, keep_ref)):
        r = block_rows(place[0], at)
        total = lax.dot_general(grad_0[r, :], weight_0[...], NT, preferred_element_type=F32)
        total += lax.dot_general(grad_1[r, :], weight_1[...], NT, preferred_element_type=F32)
        ref[...] = total.astype(ref.dtype)


def norm_grad_blocks(keep_at, give_at, place, grads, weights):
    shape = (ROWS, weights[0].shape[0])
    body = lambda *refs: norm_grad_kernel(keep_at, give_at, *refs)
    return pl.pallas_call(
        body,
        out_shape=(jax.ShapeDtypeStruct(shape, F32), jax.ShapeDtypeStruct(shape, BF16)),
        in_specs=[SM] + [VM] * 4,
        out_specs=(VM, VM),
        compiler_params=pltpu.CompilerParams(vmem_limit_bytes=10 << 20),
        cost_estimate=pl.CostEstimate(flops=1_300_000_000, bytes_accessed=6_000_000, transcendentals=0),
        name="norm_grad",
    )(place, *grads, *weights)


CHUNKS = ((2, 3, 4), (0, 1))


def pack_columns(weight, heads):
    return jnp.concatenate([weight[:, c, HD * h:HD * h + HD] for c, h in chunk_blocks(heads)], axis=1)


def unpack_columns(chunks):
    place = {}
    for heads, packed in zip(CHUNKS, chunks):
        for i, block in enumerate(chunk_blocks(heads)):
            place[block] = packed[:, HD * i:HD * i + HD]
    parts = [jnp.concatenate([place[c, h] for h in range(len(KEY_UPPER))], axis=1) for c in range(3)]
    return jnp.stack(parts, axis=1)


def plane_groups(groups):
    return [list(range(first, groups, 2)) for first in range(2)]


def swap_pair(block):
    groups = lax.axis_size("dp")
    return lax.ppermute(block, "dp", [(i, i ^ 1) for i in range(groups)])


def gather_plane(block):
    groups = lax.axis_size("dp")
    spread = lax.all_to_all(
        jnp.broadcast_to(block[None], (groups // 2,) + block.shape), "dp", 0, 0,
        axis_index_groups=plane_groups(groups), tiled=True,
    )
    return spread.reshape(groups // 2 * block.shape[0], block.shape[1])


def exchange_terms(term):
    groups = lax.axis_size("dp")
    return lax.all_to_all(
        term.reshape(groups // 2, term.shape[0] * 2 // groups, term.shape[1]), "dp", 0, 0,
        axis_index_groups=plane_groups(groups), tiled=True,
    )


def sum_terms(terms):
    second = lax.axis_index("dp") % 2
    total = jnp.sum(terms.astype(F32), axis=0)
    halves = total.reshape(2, total.shape[0] // 2, total.shape[1])
    keep = lax.dynamic_index_in_dim(halves, second, 0, keepdims=False)
    give = lax.dynamic_index_in_dim(halves, 1 - second, 0, keepdims=False)
    got = swap_pair(give.astype(BF16))
    return keep + got.astype(F32)


def grad_tiles(out_grad):
    empty = jnp.zeros((out_grad.shape[0], HD), out_grad.dtype)
    return jnp.concatenate([out_grad[:, :256], empty, out_grad[:, 256:]], axis=1)


FRAME_SIDE = [(0, 2), (1, 3), (2, 0), (3, 1)]
FRAME_CORE = [(0, 1), (1, 0), (2, 3), (3, 2)]


def swap_side(block):
    return lax.ppermute(block, "frame", FRAME_SIDE)


def swap_core(block):
    return lax.ppermute(block, "frame", FRAME_CORE)


def per_device(
    hidden_in, rec_lengths, token_positions, thinker_grad, norm_gain, norm_bias, qkv_weight
):
    head_cols = qkv_weight.shape[2]
    think_rows = thinker_grad.shape[0]
    place = lax.axis_index("frame")
    side, core = place // 2, place % 2
    shard = jnp.concatenate([pack_columns(qkv_weight, heads) for heads in CHUNKS], axis=1)
    other = swap_pair(shard)
    both = jnp.where(lax.axis_index("dp") % 2 == 0, jnp.concatenate([shard, other]), jnp.concatenate([other, shard]))
    cut = HD * len(chunk_blocks(CHUNKS[0]))
    shards = [both[:, :cut], both[:, cut:]]
    weights = [gather_plane(shards[0])]
    own, standard, inv_std = norm_forward(hidden_in, norm_gain, norm_bias)
    far = swap_side(own)
    near = swap_core(own)
    sides = [lax.dynamic_slice_in_dim(thinker_grad, 2 * head_cols * at, 2 * head_cols, 1) for at in (side, 1 - side)]
    far_think = swap_side(sides[1])
    cols = lambda block, at: lax.dynamic_slice_in_dim(block, head_cols * at, head_cols, 1)
    near_think = swap_core(cols(sides[0], 1 - core))
    far_near = swap_core(far)
    far_near_think = swap_core(cols(far_think, 1 - core))
    shard, weights[0] = lax.optimization_barrier((shards[1], weights[0]))
    weights.append(gather_plane(shard))
    moved = jnp.concatenate([cols(sides[0], core), near_think, cols(far_think, core), far_near_think], axis=0)
    rows_at = ((token_positions // think_rows) ^ place) * think_rows + token_positions % think_rows
    out_grad = grad_tiles(jnp.take(moved, rows_at, axis=0))
    pieces = (own, near, far, far_near)
    at = place.reshape(1)
    grads, terms = [], []
    for heads, weight in zip(CHUNKS, weights):
        grad, term = attention(heads, rec_lengths[0], at, pieces, weight, out_grad)
        grads.append(grad)
        terms.append(exchange_terms(term))
    keep, give = norm_grad_blocks(2, 3, at, grads, weights)
    got = swap_core(give)
    side_sum = swap_side((keep + got.astype(F32)).astype(BF16))
    keep, give = norm_grad_blocks(0, 1, at, grads, weights)
    core_sum = swap_core(give)
    norm_grad = keep + core_sum.astype(F32) + side_sum.astype(F32)
    weight_grad = unpack_columns([sum_terms(term) for term in terms])
    hidden_grad = norm_backward(norm_grad, standard, inv_std, norm_gain)
    return (hidden_grad, weight_grad)


def solution(mesh):
    placed = (
        P(("dp", "frame"), None),
        P("dp", None),
        P("dp"),
        P(("dp", "frame"), None),
        P(),
        P(),
        P("dp", None, "frame"),
    )

    return jax.shard_map(
        per_device,
        mesh=mesh,
        in_specs=placed,
        out_specs=(P(("dp", "frame"), None), P("dp", None, "frame")),
        check_vma=False,
    )
```

```python
import jax
import jax.numpy as jnp
from jax import lax
from jax.experimental import pallas as pl
from jax.experimental.pallas import tpu as pltpu
from jax.sharding import PartitionSpec as P


HD = 64


norm_eps = 1e-05


def norm_forward(rows, gain, bias):
    rows_f32 = rows.astype(jnp.float32)
    mean_row = jnp.mean(rows_f32, axis=-1, keepdims=True)
    centered = rows_f32 - mean_row
    variance = jnp.mean(centered * centered, axis=-1, keepdims=True)
    inv_std = lax.rsqrt(variance + norm_eps)
    standard = centered * inv_std
    normalized = (standard * gain + bias).astype(jnp.bfloat16)
    return (normalized, standard, inv_std)


def norm_backward(norm_grad, standard, inv_std, gain):
    scaled = norm_grad * gain
    result = inv_std * (
        scaled
        - jnp.mean(scaled, axis=-1, keepdims=True)
        - standard * jnp.mean(scaled * standard, axis=-1, keepdims=True)
    )
    return result.astype(jnp.bfloat16)


NEG = -1e30
F32 = jnp.float32
BF16 = jnp.bfloat16
QB = 256
KT = 256
ROWS = 256

KEY_UPPER = (True, False, True, False, False)
NT = (((1,), (1,)), ((), ()))
TN = (((0,), (0,)), ((), ()))


def chunk_blocks(heads):
    blocks = []
    for h in heads:
        blocks += [(2, h), (1, h)] if KEY_UPPER[h] else [(1, h), (2, h)]
    for h in heads:
        if h % 2 == 0:
            blocks += [(0, h + 1), (0, h)] if h + 1 in heads else [(0, h)]
    return tuple(blocks)


def block_rows(place, j):
    return pl.ds(pl.multiple_of((place ^ j) * ROWS, ROWS), ROWS)


def attention_kernel(
    heads, lengths, place, own, near, far, far_near, weight_ref, grad_ref, out_ref, term_ref,
    norm_ref, q_aug, q_pad, k_aug, k_pad, v_pad, g_pad, score, dprob, kv_acc, dq_acc,
):
    rows = norm_ref.shape[0]
    first_end = lengths[0]
    second_end = first_end + lengths[1]
    for j, piece in enumerate((own, near, far, far_near)):
        norm_ref[block_rows(place[0], j), :] = piece[...]
    count = len(heads)
    width = weight_ref.shape[1]
    scale = HD ** (-0.5)

    def prepare(i, carry):
        r = pl.ds(pl.multiple_of(i * ROWS, ROWS), ROWS)
        lane = lax.broadcasted_iota(jnp.int32, (ROWS, 128), 1)
        frame = i * ROWS + lax.broadcasted_iota(jnp.int32, (ROWS, 128), 0)
        seg = (frame >= first_end).astype(jnp.int32) + (frame >= second_end).astype(jnp.int32)
        proj = jnp.dot(norm_ref[r, :], weight_ref[...], preferred_element_type=F32)
        proj = proj.astype(BF16).astype(F32)
        for n, h in enumerate(heads):
            upper = KEY_UPPER[h]
            own = (lane >= 64) if upper else (lane < 64)
            slot = lane if upper else lane - 64
            kv = proj[:, 128 * n:128 * (n + 1)]
            at = 128 * (count + n // 2)
            if at + 128 <= width:
                q = proj[:, at:at + 128]
            else:
                q = jnp.concatenate([proj[:, at:at + 64], jnp.zeros((ROWS, 64), F32)], axis=1)
            q = q * scale
            g = grad_ref[r, 128 * (h // 2):128 * (h // 2) + 128].astype(F32)
            hit = slot == seg
            q_aug[n, r, :] = jnp.where(own, q, jnp.where(hit, 1.0, 0.0)).astype(BF16)
            q_pad[n, r, :] = jnp.where(own, q, 0.0).astype(BF16)
            miss = jnp.logical_and(jnp.logical_and(slot >= 0, slot < 3), jnp.logical_not(hit))
            k_aug[n, r, :] = jnp.where(own, kv, jnp.where(miss, NEG, 0.0)).astype(BF16)
            k_pad[n, r, :] = jnp.where(own, kv, 0.0).astype(BF16)
            v_pad[n, r, :] = jnp.where(own, 0.0, kv).astype(BF16)
            g_pad[n, r, :] = jnp.where(own, 0.0, g).astype(BF16)
            kv_acc[n, r, :] = jnp.zeros((ROWS, 128), F32)
        return carry

    lax.fori_loop(0, rows // ROWS, prepare, 0)

    def query_block(qb, carry):
        qr = pl.ds(pl.multiple_of(qb * QB, QB), QB)
        head_row, tail_row = qb * QB, qb * QB + (QB - 1)
        start = jnp.where(head_row >= second_end, second_end, jnp.where(head_row >= first_end, first_end, 0))
        end = jnp.where(tail_row >= second_end, rows, jnp.where(tail_row >= first_end, second_end, first_end))
        lo, hi = start // KT, (end + (KT - 1)) // KT

        def first(t, tops):
            kr = pl.ds(pl.multiple_of(t * KT, KT), KT)
            new = []
            for h in range(count):
                s = lax.dot_general(k_aug[h, kr, :], q_aug[h, qr, :], NT, preferred_element_type=F32)
                score[h, kr, :] = s
                new.append(jnp.maximum(tops[h], jnp.max(s.reshape(KT // 8, 8, QB), axis=0)))
            return tuple(new)

        tops = lax.fori_loop(lo, hi, first, tuple(jnp.full((8, QB), -3e38, F32) for _ in range(count)))
        tops = [jnp.max(x, axis=0, keepdims=True) for x in tops]

        def second(t, sums):
            kr = pl.ds(pl.multiple_of(t * KT, KT), KT)
            new = []
            for h in range(count):
                e = jnp.exp(score[h, kr, :] - tops[h])
                d = lax.dot_general(v_pad[h, kr, :], g_pad[h, qr, :], NT, preferred_element_type=F32)
                score[h, kr, :] = e
                dprob[h, kr, :] = d
                total, dotted = sums[h]
                new.append((
                    total + jnp.sum(e.reshape(KT // 8, 8, QB), axis=0),
                    dotted + jnp.sum((e * d).reshape(KT // 8, 8, QB), axis=0),
                ))
            return tuple(new)

        zero = jnp.zeros((8, QB), F32)
        sums = lax.fori_loop(lo, hi, second, tuple((zero, zero) for _ in range(count)))
        inv, dot = [], []
        for total, dotted in sums:
            one = 1.0 / jnp.sum(total, axis=0, keepdims=True)
            inv.append(one)
            dot.append(jnp.sum(dotted, axis=0, keepdims=True) * one)
        dq_acc[...] = jnp.zeros(dq_acc.shape, F32)

        def third(t, carry):
            kr = pl.ds(pl.multiple_of(t * KT, KT), KT)
            for h in range(count):
                a = score[h, kr, :] * inv[h]
                ds = (a * (dprob[h, kr, :] - dot[h])).astype(BF16)
                w = a.astype(BF16)
                kv_acc[h, kr, :] += (
                    jnp.dot(ds, q_pad[h, qr, :], preferred_element_type=F32)
                    + jnp.dot(w, g_pad[h, qr, :], preferred_element_type=F32)
                )
                dq_acc[h // 2] += lax.dot_general(ds, k_pad[h, kr, :], TN, preferred_element_type=F32)
            return carry

        lax.fori_loop(lo, hi, third, 0)
        for p in range((count + 1) // 2):
            at = 128 * (count + p)
            span = min(128, width - at)
            out_ref[qr, at:at + span] = (dq_acc[p] * scale).astype(BF16)[:, :span]
        return carry

    lax.fori_loop(0, rows // QB, query_block, 0)

    def finish(i, carry):
        r = pl.ds(pl.multiple_of(i * ROWS, ROWS), ROWS)
        for h in range(count):
            out_ref[r, 128 * h:128 * (h + 1)] = kv_acc[h, r, :].astype(BF16)
        return carry

    lax.fori_loop(0, rows // ROWS, finish, 0)

    for i in range(norm_ref.shape[1] // 256):
        part = lax.dot_general(norm_ref[:, 256 * i:256 * i + 256], out_ref[...], TN, preferred_element_type=F32)
        term_ref[256 * i:256 * i + 256, :] = part.astype(BF16)


VM = pl.BlockSpec(memory_space=pltpu.VMEM)
SM = pl.BlockSpec(memory_space=pltpu.SMEM)


def attention(heads, lengths, place, pieces, weight, out_grad):
    features, columns = weight.shape
    rows = out_grad.shape[0]
    count = len(heads)
    tall = pltpu.VMEM((count, rows, 128), BF16)
    wide = pltpu.VMEM((count, rows, QB), F32)
    body = lambda *refs: attention_kernel(heads, *refs)
    return pl.pallas_call(
        body,
        out_shape=(
            jax.ShapeDtypeStruct((rows, columns), BF16),
            jax.ShapeDtypeStruct((features, columns), BF16),
        ),
        in_specs=[SM, SM] + [VM] * 6,
        out_specs=(VM, VM),
        scratch_shapes=[pltpu.VMEM((rows, features), BF16)] + [tall] * 6 + [
            wide, wide, pltpu.VMEM((count, rows, 128), F32), pltpu.VMEM(((count + 1) // 2, QB, 128), F32)
        ],
        compiler_params=pltpu.CompilerParams(vmem_limit_bytes=(12 + 5 * count) << 20),
        cost_estimate=pl.CostEstimate(
            flops=5_000_000_000 * count, bytes_accessed=8_000_000, transcendentals=1_000_000 * count
        ),
        name="attention_backward",
    )(lengths, place, *pieces, weight, out_grad)


def norm_grad_kernel(keep_at, give_at, place, grad_0, grad_1, weight_0, weight_1, keep_ref, give_ref):
    for at, ref in ((give_at, give_ref), (keep_at, keep_ref)):
        r = block_rows(place[0], at)
        total = lax.dot_general(grad_0[r, :], weight_0[...], NT, preferred_element_type=F32)
        total += lax.dot_general(grad_1[r, :], weight_1[...], NT, preferred_element_type=F32)
        ref[...] = total.astype(ref.dtype)


def norm_grad_blocks(keep_at, give_at, place, grads, weights):
    shape = (ROWS, weights[0].shape[0])
    body = lambda *refs: norm_grad_kernel(keep_at, give_at, *refs)
    return pl.pallas_call(
        body,
        out_shape=(jax.ShapeDtypeStruct(shape, F32), jax.ShapeDtypeStruct(shape, BF16)),
        in_specs=[SM] + [VM] * 4,
        out_specs=(VM, VM),
        compiler_params=pltpu.CompilerParams(vmem_limit_bytes=10 << 20),
        cost_estimate=pl.CostEstimate(flops=1_300_000_000, bytes_accessed=6_000_000, transcendentals=0),
        name="norm_grad",
    )(place, *grads, *weights)


CHUNKS = ((2, 3, 4), (0, 1))


def pack_columns(weight, heads):
    return jnp.concatenate([weight[:, c, HD * h:HD * h + HD] for c, h in chunk_blocks(heads)], axis=1)


def unpack_columns(chunks):
    place = {}
    for heads, packed in zip(CHUNKS, chunks):
        for i, block in enumerate(chunk_blocks(heads)):
            place[block] = packed[:, HD * i:HD * i + HD]
    parts = [jnp.concatenate([place[c, h] for h in range(len(KEY_UPPER))], axis=1) for c in range(3)]
    return jnp.stack(parts, axis=1)


def plane_groups(groups):
    return [list(range(first, groups, 2)) for first in range(2)]


def swap_pair(block):
    groups = lax.axis_size("dp")
    return lax.ppermute(block, "dp", [(i, i ^ 1) for i in range(groups)])


def spread_plane(block):
    return jnp.broadcast_to(block[None], (lax.axis_size("dp") // 2,) + block.shape)


def gather_plane(spread):
    groups = lax.axis_size("dp")
    got = lax.all_to_all(spread, "dp", 0, 0, axis_index_groups=plane_groups(groups), tiled=True)
    return got.reshape(got.shape[0] * got.shape[1], got.shape[2])


def exchange_terms(term):
    groups = lax.axis_size("dp")
    return lax.all_to_all(
        term.reshape(groups // 2, term.shape[0] * 2 // groups, term.shape[1]), "dp", 0, 0,
        axis_index_groups=plane_groups(groups), tiled=True,
    )


def sum_terms(terms):
    second = lax.axis_index("dp") % 2
    total = jnp.sum(terms.astype(F32), axis=0)
    halves = total.reshape(2, total.shape[0] // 2, total.shape[1])
    keep = lax.dynamic_index_in_dim(halves, second, 0, keepdims=False)
    give = lax.dynamic_index_in_dim(halves, 1 - second, 0, keepdims=False)
    got = swap_pair(give.astype(BF16))
    return keep + got.astype(F32)


def grad_tiles(out_grad):
    empty = jnp.zeros((out_grad.shape[0], HD), out_grad.dtype)
    return jnp.concatenate([out_grad[:, :256], empty, out_grad[:, 256:]], axis=1)


FRAME_SIDE = [(0, 2), (1, 3), (2, 0), (3, 1)]
FRAME_CORE = [(0, 1), (1, 0), (2, 3), (3, 2)]


def swap_side(block):
    return lax.ppermute(block, "frame", FRAME_SIDE)


def swap_core(block):
    return lax.ppermute(block, "frame", FRAME_CORE)


def per_device(
    hidden_in, rec_lengths, token_positions, thinker_grad, norm_gain, norm_bias, qkv_weight
):
    head_cols = qkv_weight.shape[2]
    think_rows = thinker_grad.shape[0]
    place = lax.axis_index("frame")
    side, core = place // 2, place % 2
    shard = jnp.concatenate([pack_columns(qkv_weight, heads) for heads in CHUNKS], axis=1)
    other = swap_pair(shard)
    both = jnp.where(lax.axis_index("dp") % 2 == 0, jnp.concatenate([shard, other]), jnp.concatenate([other, shard]))
    cut = HD * len(chunk_blocks(CHUNKS[0]))
    shards = [spread_plane(both[:, :cut])]
    shards.append(spread_plane(both[:, cut:]))
    weights = [gather_plane(shards[0])]
    own, standard, inv_std = norm_forward(hidden_in, norm_gain, norm_bias)
    far = swap_side(own)
    near = swap_core(own)
    sides = [lax.dynamic_slice_in_dim(thinker_grad, 2 * head_cols * at, 2 * head_cols, 1) for at in (side, 1 - side)]
    far_think = swap_side(sides[1])
    cols = lambda block, at: lax.dynamic_slice_in_dim(block, head_cols * at, head_cols, 1)
    near_half, own_half = cols(sides[0], 1 - core), cols(sides[0], core)
    near_think = swap_core(near_half)
    far_near = swap_core(far)
    far_near_think = swap_core(cols(far_think, 1 - core))
    shard, weights[0] = lax.optimization_barrier((shards[1], weights[0]))
    weights.append(gather_plane(shard))
    moved = jnp.concatenate([own_half, near_think, cols(far_think, core), far_near_think], axis=0)
    rows_at = ((token_positions // think_rows) ^ place) * think_rows + token_positions % think_rows
    out_grad = grad_tiles(jnp.take(moved, rows_at, axis=0, mode="clip"))
    pieces = (own, near, far, far_near)
    at = place.reshape(1)
    grads, terms = [], []
    for heads, weight in zip(CHUNKS, weights):
        grad, term = attention(heads, rec_lengths[0], at, pieces, weight, out_grad)
        grads.append(grad)
        terms.append(exchange_terms(term))
    keep, give = norm_grad_blocks(2, 3, at, grads, weights)
    got = swap_core(give)
    side_sum = swap_side((keep + got.astype(F32)).astype(BF16))
    keep, give = norm_grad_blocks(0, 1, at, grads, weights)
    core_sum = swap_core(give)
    norm_grad = keep + core_sum.astype(F32) + side_sum.astype(F32)
    weight_grad = unpack_columns([sum_terms(term) for term in terms])
    hidden_grad = norm_backward(norm_grad, standard, inv_std, norm_gain)
    return (hidden_grad, weight_grad)


def solution(mesh):
    placed = (
        P(("dp", "frame"), None),
        P("dp", None),
        P("dp"),
        P(("dp", "frame"), None),
        P(),
        P(),
        P("dp", None, "frame"),
    )

    return jax.shard_map(
        per_device,
        mesh=mesh,
        in_specs=placed,
        out_specs=(P(("dp", "frame"), None), P("dp", None, "frame")),
        check_vma=False,
    )
```

```python
import jax
import jax.numpy as jnp
from jax import lax
from jax.experimental import pallas as pl
from jax.experimental.pallas import tpu as pltpu
from jax.sharding import PartitionSpec as P


HD = 64


norm_eps = 1e-05


def norm_forward(rows, gain, bias):
    rows_f32 = rows.astype(jnp.float32)
    mean_row = jnp.mean(rows_f32, axis=-1, keepdims=True)
    centered = rows_f32 - mean_row
    variance = jnp.mean(centered * centered, axis=-1, keepdims=True)
    inv_std = lax.rsqrt(variance + norm_eps)
    standard = centered * inv_std
    normalized = (standard * gain + bias).astype(jnp.bfloat16)
    return (normalized, standard, inv_std)


def norm_backward(norm_grad, standard, inv_std, gain):
    scaled = norm_grad * gain
    result = inv_std * (
        scaled
        - jnp.mean(scaled, axis=-1, keepdims=True)
        - standard * jnp.mean(scaled * standard, axis=-1, keepdims=True)
    )
    return result.astype(jnp.bfloat16)


NEG = -1e30
F32 = jnp.float32
BF16 = jnp.bfloat16
QB = 256
KT = 256
ROWS = 256

KEY_UPPER = (True, False, True, False, False)
NT = (((1,), (1,)), ((), ()))
TN = (((0,), (0,)), ((), ()))


def chunk_blocks(heads):
    blocks = []
    for h in heads:
        blocks += [(2, h), (1, h)] if KEY_UPPER[h] else [(1, h), (2, h)]
    for h in heads:
        if h % 2 == 0:
            blocks += [(0, h + 1), (0, h)] if h + 1 in heads else [(0, h)]
    return tuple(blocks)


def block_rows(place, j):
    return pl.ds(pl.multiple_of((place ^ j) * ROWS, ROWS), ROWS)


def attention_kernel(
    heads, lengths, place, own, near, far, far_near, weight_ref, grad_ref, out_ref, term_ref,
    norm_ref, q_aug, q_pad, k_aug, k_pad, v_pad, g_pad, score, dprob, kv_acc, dq_acc,
):
    rows = norm_ref.shape[0]
    first_end = lengths[0]
    second_end = first_end + lengths[1]
    for j, piece in enumerate((own, near, far, far_near)):
        norm_ref[block_rows(place[0], j), :] = piece[...]
    count = len(heads)
    width = weight_ref.shape[1]
    scale = HD ** (-0.5)

    def prepare(i, carry):
        r = pl.ds(pl.multiple_of(i * ROWS, ROWS), ROWS)
        lane = lax.broadcasted_iota(jnp.int32, (ROWS, 128), 1)
        frame = i * ROWS + lax.broadcasted_iota(jnp.int32, (ROWS, 128), 0)
        seg = (frame >= first_end).astype(jnp.int32) + (frame >= second_end).astype(jnp.int32)
        proj = jnp.dot(norm_ref[r, :], weight_ref[...], preferred_element_type=F32)
        proj = proj.astype(BF16).astype(F32)
        for n, h in enumerate(heads):
            upper = KEY_UPPER[h]
            own = (lane >= 64) if upper else (lane < 64)
            slot = lane if upper else lane - 64
            kv = proj[:, 128 * n:128 * (n + 1)]
            at = 128 * (count + n // 2)
            if at + 128 <= width:
                q = proj[:, at:at + 128]
            else:
                q = jnp.concatenate([proj[:, at:at + 64], jnp.zeros((ROWS, 64), F32)], axis=1)
            q = q * scale
            g = grad_ref[r, 128 * (h // 2):128 * (h // 2) + 128].astype(F32)
            hit = slot == seg
            q_aug[n, r, :] = jnp.where(own, q, jnp.where(hit, 1.0, 0.0)).astype(BF16)
            q_pad[n, r, :] = jnp.where(own, q, 0.0).astype(BF16)
            miss = jnp.logical_and(jnp.logical_and(slot >= 0, slot < 3), jnp.logical_not(hit))
            k_aug[n, r, :] = jnp.where(own, kv, jnp.where(miss, NEG, 0.0)).astype(BF16)
            k_pad[n, r, :] = jnp.where(own, kv, 0.0).astype(BF16)
            v_pad[n, r, :] = jnp.where(own, 0.0, kv).astype(BF16)
            g_pad[n, r, :] = jnp.where(own, 0.0, g).astype(BF16)
            kv_acc[n, r, :] = jnp.zeros((ROWS, 128), F32)
        return carry

    lax.fori_loop(0, rows // ROWS, prepare, 0)

    def query_block(qb, carry):
        qr = pl.ds(pl.multiple_of(qb * QB, QB), QB)
        head_row, tail_row = qb * QB, qb * QB + (QB - 1)
        start = jnp.where(head_row >= second_end, second_end, jnp.where(head_row >= first_end, first_end, 0))
        end = jnp.where(tail_row >= second_end, rows, jnp.where(tail_row >= first_end, second_end, first_end))
        lo, hi = start // KT, (end + (KT - 1)) // KT

        def first(t, tops):
            kr = pl.ds(pl.multiple_of(t * KT, KT), KT)
            new = []
            for h in range(count):
                s = lax.dot_general(k_aug[h, kr, :], q_aug[h, qr, :], NT, preferred_element_type=F32)
                score[h, kr, :] = s
                new.append(jnp.maximum(tops[h], jnp.max(s.reshape(KT // 8, 8, QB), axis=0)))
            return tuple(new)

        tops = lax.fori_loop(lo, hi, first, tuple(jnp.full((8, QB), -3e38, F32) for _ in range(count)))
        tops = [jnp.max(x, axis=0, keepdims=True) for x in tops]

        def second(t, sums):
            kr = pl.ds(pl.multiple_of(t * KT, KT), KT)
            new = []
            for h in range(count):
                e = jnp.exp(score[h, kr, :] - tops[h])
                d = lax.dot_general(v_pad[h, kr, :], g_pad[h, qr, :], NT, preferred_element_type=F32)
                score[h, kr, :] = e
                dprob[h, kr, :] = d
                total, dotted = sums[h]
                new.append((
                    total + jnp.sum(e.reshape(KT // 8, 8, QB), axis=0),
                    dotted + jnp.sum((e * d).reshape(KT // 8, 8, QB), axis=0),
                ))
            return tuple(new)

        zero = jnp.zeros((8, QB), F32)
        sums = lax.fori_loop(lo, hi, second, tuple((zero, zero) for _ in range(count)))
        inv, dot = [], []
        for total, dotted in sums:
            one = 1.0 / jnp.sum(total, axis=0, keepdims=True)
            inv.append(one)
            dot.append(jnp.sum(dotted, axis=0, keepdims=True) * one)
        dq_acc[...] = jnp.zeros(dq_acc.shape, F32)

        def third(t, carry):
            kr = pl.ds(pl.multiple_of(t * KT, KT), KT)
            for h in range(count):
                a = score[h, kr, :] * inv[h]
                ds = (a * (dprob[h, kr, :] - dot[h])).astype(BF16)
                w = a.astype(BF16)
                kv_acc[h, kr, :] += (
                    jnp.dot(ds, q_pad[h, qr, :], preferred_element_type=F32)
                    + jnp.dot(w, g_pad[h, qr, :], preferred_element_type=F32)
                )
                dq_acc[h // 2] += lax.dot_general(ds, k_pad[h, kr, :], TN, preferred_element_type=F32)
            return carry

        lax.fori_loop(lo, hi, third, 0)
        for p in range((count + 1) // 2):
            at = 128 * (count + p)
            span = min(128, width - at)
            out_ref[qr, at:at + span] = (dq_acc[p] * scale).astype(BF16)[:, :span]
        return carry

    lax.fori_loop(0, rows // QB, query_block, 0)

    def finish(i, carry):
        r = pl.ds(pl.multiple_of(i * ROWS, ROWS), ROWS)
        for h in range(count):
            out_ref[r, 128 * h:128 * (h + 1)] = kv_acc[h, r, :].astype(BF16)
        return carry

    lax.fori_loop(0, rows // ROWS, finish, 0)

    for i in range(norm_ref.shape[1] // 256):
        part = lax.dot_general(norm_ref[:, 256 * i:256 * i + 256], out_ref[...], TN, preferred_element_type=F32)
        term_ref[256 * i:256 * i + 256, :] = part.astype(BF16)


VM = pl.BlockSpec(memory_space=pltpu.VMEM)
SM = pl.BlockSpec(memory_space=pltpu.SMEM)


def attention(heads, lengths, place, pieces, weight, out_grad):
    features, columns = weight.shape
    rows = out_grad.shape[0]
    count = len(heads)
    tall = pltpu.VMEM((count, rows, 128), BF16)
    wide = pltpu.VMEM((count, rows, QB), F32)
    body = lambda *refs: attention_kernel(heads, *refs)
    return pl.pallas_call(
        body,
        out_shape=(
            jax.ShapeDtypeStruct((rows, columns), BF16),
            jax.ShapeDtypeStruct((features, columns), BF16),
        ),
        in_specs=[SM, SM] + [VM] * 6,
        out_specs=(VM, VM),
        scratch_shapes=[pltpu.VMEM((rows, features), BF16)] + [tall] * 6 + [
            wide, wide, pltpu.VMEM((count, rows, 128), F32), pltpu.VMEM(((count + 1) // 2, QB, 128), F32)
        ],
        compiler_params=pltpu.CompilerParams(vmem_limit_bytes=(12 + 5 * count) << 20),
        cost_estimate=pl.CostEstimate(
            flops=5_000_000_000 * count, bytes_accessed=8_000_000, transcendentals=1_000_000 * count
        ),
        name="attention_backward",
    )(lengths, place, *pieces, weight, out_grad)


def norm_grad_kernel(keep_at, give_at, place, grad_0, grad_1, weight_0, weight_1, keep_ref, give_ref):
    for at, ref in ((give_at, give_ref), (keep_at, keep_ref)):
        r = block_rows(place[0], at)
        total = lax.dot_general(grad_0[r, :], weight_0[...], NT, preferred_element_type=F32)
        total += lax.dot_general(grad_1[r, :], weight_1[...], NT, preferred_element_type=F32)
        ref[...] = total.astype(ref.dtype)


def norm_grad_blocks(keep_at, give_at, place, grads, weights):
    features = weights[0].shape[0]
    shape = (ROWS, features)
    body = lambda *refs: norm_grad_kernel(keep_at, give_at, *refs)
    out_block = pl.BlockSpec((ROWS, 256), lambda i: (0, i))
    return pl.pallas_call(
        body,
        grid=(features // 256,),
        out_shape=(jax.ShapeDtypeStruct(shape, F32), jax.ShapeDtypeStruct(shape, BF16)),
        in_specs=[SM] + [pl.BlockSpec(grad.shape, lambda i: (0, 0)) for grad in grads] + [
            pl.BlockSpec((256, weight.shape[1]), lambda i: (i, 0)) for weight in weights
        ],
        out_specs=(out_block, out_block),
        compiler_params=pltpu.CompilerParams(vmem_limit_bytes=10 << 20),
        cost_estimate=pl.CostEstimate(flops=1_300_000_000, bytes_accessed=6_000_000, transcendentals=0),
        name="norm_grad",
    )(place, *grads, *weights)


CHUNKS = ((2, 3, 4), (0, 1))


def pack_columns(weight, heads):
    return jnp.concatenate([weight[:, c, HD * h:HD * h + HD] for c, h in chunk_blocks(heads)], axis=1)


def unpack_columns(chunks):
    place = {}
    for heads, packed in zip(CHUNKS, chunks):
        for i, block in enumerate(chunk_blocks(heads)):
            place[block] = packed[:, HD * i:HD * i + HD]
    parts = [jnp.concatenate([place[c, h] for h in range(len(KEY_UPPER))], axis=1) for c in range(3)]
    return jnp.stack(parts, axis=1)


def plane_groups(groups):
    return [list(range(first, groups, 2)) for first in range(2)]


def swap_pair(block):
    groups = lax.axis_size("dp")
    return lax.ppermute(block, "dp", [(i, i ^ 1) for i in range(groups)])


def spread_plane(block):
    return jnp.broadcast_to(block[None], (lax.axis_size("dp") // 2,) + block.shape)


def gather_plane(spread):
    groups = lax.axis_size("dp")
    got = lax.all_to_all(spread, "dp", 0, 0, axis_index_groups=plane_groups(groups), tiled=True)
    return got.reshape(got.shape[0] * got.shape[1], got.shape[2])


def exchange_terms(term):
    groups = lax.axis_size("dp")
    return lax.all_to_all(
        term.reshape(groups // 2, term.shape[0] * 2 // groups, term.shape[1]), "dp", 0, 0,
        axis_index_groups=plane_groups(groups), tiled=True,
    )


def sum_terms(terms):
    second = lax.axis_index("dp") % 2
    total = jnp.sum(terms.astype(F32), axis=0)
    halves = total.reshape(2, total.shape[0] // 2, total.shape[1])
    keep = lax.dynamic_index_in_dim(halves, second, 0, keepdims=False)
    give = lax.dynamic_index_in_dim(halves, 1 - second, 0, keepdims=False)
    got = swap_pair(give.astype(BF16))
    return keep + got.astype(F32)


def grad_tiles(out_grad):
    empty = jnp.zeros((out_grad.shape[0], HD), out_grad.dtype)
    return jnp.concatenate([out_grad[:, :256], empty, out_grad[:, 256:]], axis=1)


FRAME_SIDE = [(0, 2), (1, 3), (2, 0), (3, 1)]
FRAME_CORE = [(0, 1), (1, 0), (2, 3), (3, 2)]


def swap_side(block):
    return lax.ppermute(block, "frame", FRAME_SIDE)


def swap_core(block):
    return lax.ppermute(block, "frame", FRAME_CORE)


def per_device(
    hidden_in, rec_lengths, token_positions, thinker_grad, norm_gain, norm_bias, qkv_weight
):
    head_cols = qkv_weight.shape[2]
    think_rows = thinker_grad.shape[0]
    place = lax.axis_index("frame")
    side, core = place // 2, place % 2
    shard = jnp.concatenate([pack_columns(qkv_weight, heads) for heads in CHUNKS], axis=1)
    other = swap_pair(shard)
    both = jnp.where(lax.axis_index("dp") % 2 == 0, jnp.concatenate([shard, other]), jnp.concatenate([other, shard]))
    cut = HD * len(chunk_blocks(CHUNKS[0]))
    shards = [spread_plane(both[:, :cut])]
    shards.append(spread_plane(both[:, cut:]))
    weights = [gather_plane(shards[0])]
    own, standard, inv_std = norm_forward(hidden_in, norm_gain, norm_bias)
    far = swap_side(own)
    near = swap_core(own)
    sides = [lax.dynamic_slice_in_dim(thinker_grad, 2 * head_cols * at, 2 * head_cols, 1) for at in (side, 1 - side)]
    far_think = swap_side(sides[1])
    cols = lambda block, at: lax.dynamic_slice_in_dim(block, head_cols * at, head_cols, 1)
    near_half, own_half = cols(sides[0], 1 - core), cols(sides[0], core)
    near_think = swap_core(near_half)
    far_near = swap_core(far)
    far_near_think = swap_core(cols(far_think, 1 - core))
    shard, weights[0] = lax.optimization_barrier((shards[1], weights[0]))
    weights.append(gather_plane(shard))
    moved = jnp.concatenate([own_half, near_think, cols(far_think, core), far_near_think], axis=0)
    rows_at = ((token_positions // think_rows) ^ place) * think_rows + token_positions % think_rows
    out_grad = grad_tiles(jnp.take(moved, rows_at, axis=0, mode="clip"))
    pieces = (own, near, far, far_near)
    at = place.reshape(1)
    grads, terms = [], []
    for heads, weight in zip(CHUNKS, weights):
        grad, term = attention(heads, rec_lengths[0], at, pieces, weight, out_grad)
        grads.append(grad)
        terms.append(exchange_terms(term))
    keep, give = norm_grad_blocks(2, 3, at, grads, weights)
    got = swap_core(give)
    side_sum = swap_side((keep + got.astype(F32)).astype(BF16))
    keep, give = norm_grad_blocks(0, 1, at, grads, weights)
    core_sum = swap_core(give)
    norm_grad = keep + core_sum.astype(F32) + side_sum.astype(F32)
    weight_grad = unpack_columns([sum_terms(term) for term in terms])
    hidden_grad = norm_backward(norm_grad, standard, inv_std, norm_gain)
    return (hidden_grad, weight_grad)


def solution(mesh):
    placed = (
        P(("dp", "frame"), None),
        P("dp", None),
        P("dp"),
        P(("dp", "frame"), None),
        P(),
        P(),
        P("dp", None, "frame"),
    )

    return jax.shard_map(
        per_device,
        mesh=mesh,
        in_specs=placed,
        out_specs=(P(("dp", "frame"), None), P("dp", None, "frame")),
        check_vma=False,
    )
```

```python
import jax
import jax.numpy as jnp
from jax import lax
from jax.experimental import pallas as pl
from jax.experimental.pallas import tpu as pltpu
from jax.sharding import PartitionSpec as P


HD = 64


norm_eps = 1e-05


def norm_forward(rows, gain, bias):
    rows_f32 = rows.astype(jnp.float32)
    mean_row = jnp.mean(rows_f32, axis=-1, keepdims=True)
    centered = rows_f32 - mean_row
    variance = jnp.mean(centered * centered, axis=-1, keepdims=True)
    inv_std = lax.rsqrt(variance + norm_eps)
    standard = centered * inv_std
    normalized = (standard * gain + bias).astype(jnp.bfloat16)
    return (normalized, standard, inv_std)


def norm_backward(norm_grad, standard, inv_std, gain):
    scaled = norm_grad * gain
    result = inv_std * (
        scaled
        - jnp.mean(scaled, axis=-1, keepdims=True)
        - standard * jnp.mean(scaled * standard, axis=-1, keepdims=True)
    )
    return result.astype(jnp.bfloat16)


NEG = -1e30
F32 = jnp.float32
BF16 = jnp.bfloat16
QB = 256
KT = 256
ROWS = 256

KEY_UPPER = (True, False, True, False, False)
NT = (((1,), (1,)), ((), ()))
TN = (((0,), (0,)), ((), ()))


def chunk_blocks(heads):
    blocks = []
    for h in heads:
        blocks += [(2, h), (1, h)] if KEY_UPPER[h] else [(1, h), (2, h)]
    for h in heads:
        if h % 2 == 0:
            blocks += [(0, h + 1), (0, h)] if h + 1 in heads else [(0, h)]
    return tuple(blocks)


def block_rows(place, j):
    return pl.ds(pl.multiple_of((place ^ j) * ROWS, ROWS), ROWS)


def attention_kernel(
    heads, lengths, place, own, near, far, far_near, weight_ref, grad_ref, out_ref, term_ref,
    norm_ref, q_aug, q_pad, k_aug, k_pad, v_pad, g_pad, score, dprob, kv_acc, dq_acc,
):
    rows = norm_ref.shape[0]
    first_end = lengths[0]
    second_end = first_end + lengths[1]
    for j, piece in enumerate((own, near, far, far_near)):
        norm_ref[block_rows(place[0], j), :] = piece[...]
    count = len(heads)
    width = weight_ref.shape[1]
    scale = HD ** (-0.5)

    def prepare(i, carry):
        r = pl.ds(pl.multiple_of(i * ROWS, ROWS), ROWS)
        lane = lax.broadcasted_iota(jnp.int32, (ROWS, 128), 1)
        frame = i * ROWS + lax.broadcasted_iota(jnp.int32, (ROWS, 128), 0)
        seg = (frame >= first_end).astype(jnp.int32) + (frame >= second_end).astype(jnp.int32)
        proj = jnp.dot(norm_ref[r, :], weight_ref[...], preferred_element_type=F32)
        proj = proj.astype(BF16).astype(F32)
        for n, h in enumerate(heads):
            upper = KEY_UPPER[h]
            own = (lane >= 64) if upper else (lane < 64)
            slot = lane if upper else lane - 64
            kv = proj[:, 128 * n:128 * (n + 1)]
            at = 128 * (count + n // 2)
            if at + 128 <= width:
                q = proj[:, at:at + 128]
            else:
                q = jnp.concatenate([proj[:, at:at + 64], jnp.zeros((ROWS, 64), F32)], axis=1)
            q = q * scale
            g = grad_ref[r, 128 * (h // 2):128 * (h // 2) + 128].astype(F32)
            hit = slot == seg
            q_aug[n, r, :] = jnp.where(own, q, jnp.where(hit, 1.0, 0.0)).astype(BF16)
            q_pad[n, r, :] = jnp.where(own, q, 0.0).astype(BF16)
            miss = jnp.logical_and(jnp.logical_and(slot >= 0, slot < 3), jnp.logical_not(hit))
            k_aug[n, r, :] = jnp.where(own, kv, jnp.where(miss, NEG, 0.0)).astype(BF16)
            k_pad[n, r, :] = jnp.where(own, kv, 0.0).astype(BF16)
            v_pad[n, r, :] = jnp.where(own, 0.0, kv).astype(BF16)
            g_pad[n, r, :] = jnp.where(own, 0.0, g).astype(BF16)
            kv_acc[n, r, :] = jnp.zeros((ROWS, 128), F32)
        return carry

    lax.fori_loop(0, rows // ROWS, prepare, 0)

    def query_block(qb, carry):
        qr = pl.ds(pl.multiple_of(qb * QB, QB), QB)
        head_row, tail_row = qb * QB, qb * QB + (QB - 1)
        start = jnp.where(head_row >= second_end, second_end, jnp.where(head_row >= first_end, first_end, 0))
        end = jnp.where(tail_row >= second_end, rows, jnp.where(tail_row >= first_end, second_end, first_end))
        lo, hi = start // KT, (end + (KT - 1)) // KT

        def first(t, tops):
            kr = pl.ds(pl.multiple_of(t * KT, KT), KT)
            new = []
            for h in range(count):
                s = lax.dot_general(k_aug[h, kr, :], q_aug[h, qr, :], NT, preferred_element_type=F32)
                score[h, kr, :] = s
                new.append(jnp.maximum(tops[h], jnp.max(s.reshape(KT // 8, 8, QB), axis=0)))
            return tuple(new)

        tops = lax.fori_loop(lo, hi, first, tuple(jnp.full((8, QB), -3e38, F32) for _ in range(count)))
        tops = [jnp.max(x, axis=0, keepdims=True) for x in tops]

        def second(t, sums):
            kr = pl.ds(pl.multiple_of(t * KT, KT), KT)
            new = []
            for h in range(count):
                e = jnp.exp(score[h, kr, :] - tops[h])
                d = lax.dot_general(v_pad[h, kr, :], g_pad[h, qr, :], NT, preferred_element_type=F32)
                score[h, kr, :] = e
                dprob[h, kr, :] = d
                total, dotted = sums[h]
                new.append((
                    total + jnp.sum(e.reshape(KT // 8, 8, QB), axis=0),
                    dotted + jnp.sum((e * d).reshape(KT // 8, 8, QB), axis=0),
                ))
            return tuple(new)

        zero = jnp.zeros((8, QB), F32)
        sums = lax.fori_loop(lo, hi, second, tuple((zero, zero) for _ in range(count)))
        inv, dot = [], []
        for total, dotted in sums:
            one = 1.0 / jnp.sum(total, axis=0, keepdims=True)
            inv.append(one)
            dot.append(jnp.sum(dotted, axis=0, keepdims=True) * one)
        dq_acc[...] = jnp.zeros(dq_acc.shape, F32)

        def third(t, carry):
            kr = pl.ds(pl.multiple_of(t * KT, KT), KT)
            for h in range(count):
                a = score[h, kr, :] * inv[h]
                ds = (a * (dprob[h, kr, :] - dot[h])).astype(BF16)
                w = a.astype(BF16)
                kv_acc[h, kr, :] += (
                    jnp.dot(ds, q_pad[h, qr, :], preferred_element_type=F32)
                    + jnp.dot(w, g_pad[h, qr, :], preferred_element_type=F32)
                )
                dq_acc[h // 2] += lax.dot_general(ds, k_pad[h, kr, :], TN, preferred_element_type=F32)
            return carry

        lax.fori_loop(lo, hi, third, 0)
        for p in range((count + 1) // 2):
            at = 128 * (count + p)
            span = min(128, width - at)
            out_ref[qr, at:at + span] = (dq_acc[p] * scale).astype(BF16)[:, :span]
        return carry

    lax.fori_loop(0, rows // QB, query_block, 0)

    def finish(i, carry):
        r = pl.ds(pl.multiple_of(i * ROWS, ROWS), ROWS)
        for h in range(count):
            out_ref[r, 128 * h:128 * (h + 1)] = kv_acc[h, r, :].astype(BF16)
        return carry

    lax.fori_loop(0, rows // ROWS, finish, 0)

    for i in range(norm_ref.shape[1] // 256):
        part = lax.dot_general(norm_ref[:, 256 * i:256 * i + 256], out_ref[...], TN, preferred_element_type=F32)
        term_ref[256 * i:256 * i + 256, :] = part.astype(BF16)


VM = pl.BlockSpec(memory_space=pltpu.VMEM)
SM = pl.BlockSpec(memory_space=pltpu.SMEM)


def attention(heads, lengths, place, pieces, weight, out_grad, before=()):
    features, columns = weight.shape
    rows = out_grad.shape[0]
    count = len(heads)
    tall = pltpu.VMEM((count, rows, 128), BF16)
    wide = pltpu.VMEM((count, rows, QB), F32)
    out_shape = [
        jax.ShapeDtypeStruct((rows, columns), BF16),
        jax.ShapeDtypeStruct((features, columns), BF16),
    ]
    if before:
        out_shape += [jax.ShapeDtypeStruct((ROWS, features), F32), jax.ShapeDtypeStruct((ROWS, features), BF16)]

    def body(*refs):
        inputs, rest = refs[:8], refs[8:]
        first, rest = rest[:len(before)], rest[len(before):]
        outs, scratch = rest[:len(out_shape)], rest[len(out_shape):]
        attention_kernel(heads, *inputs, *outs[:2], *scratch)
        if before:
            norm_grad_kernel(2, 3, inputs[1], first[0], outs[0], first[1], inputs[6], *outs[2:])

    return pl.pallas_call(
        body,
        out_shape=tuple(out_shape),
        in_specs=[SM, SM] + [VM] * (6 + len(before)),
        out_specs=(VM,) * len(out_shape),
        scratch_shapes=[pltpu.VMEM((rows, features), BF16)] + [tall] * 6 + [
            wide, wide, pltpu.VMEM((count, rows, 128), F32), pltpu.VMEM(((count + 1) // 2, QB, 128), F32)
        ],
        compiler_params=pltpu.CompilerParams(vmem_limit_bytes=(12 + 5 * count + 4 * len(before)) << 20),
        cost_estimate=pl.CostEstimate(
            flops=5_000_000_000 * count, bytes_accessed=8_000_000, transcendentals=1_000_000 * count
        ),
        name="attention_backward",
    )(lengths, place, *pieces, weight, out_grad, *before)


def norm_grad_kernel(keep_at, give_at, place, grad_0, grad_1, weight_0, weight_1, keep_ref, give_ref):
    for at, ref in ((give_at, give_ref), (keep_at, keep_ref)):
        r = block_rows(place[0], at)
        total = lax.dot_general(grad_0[r, :], weight_0[...], NT, preferred_element_type=F32)
        total += lax.dot_general(grad_1[r, :], weight_1[...], NT, preferred_element_type=F32)
        ref[...] = total.astype(ref.dtype)


def norm_grad_blocks(keep_at, give_at, place, grads, weights):
    shape = (ROWS, weights[0].shape[0])
    body = lambda *refs: norm_grad_kernel(keep_at, give_at, *refs)
    return pl.pallas_call(
        body,
        out_shape=(jax.ShapeDtypeStruct(shape, F32), jax.ShapeDtypeStruct(shape, BF16)),
        in_specs=[SM] + [VM] * 4,
        out_specs=(VM, VM),
        compiler_params=pltpu.CompilerParams(vmem_limit_bytes=10 << 20),
        cost_estimate=pl.CostEstimate(flops=1_300_000_000, bytes_accessed=6_000_000, transcendentals=0),
        name="norm_grad",
    )(place, *grads, *weights)


CHUNKS = ((2, 3, 4), (0, 1))


def pack_columns(weight, heads):
    return jnp.concatenate([weight[:, c, HD * h:HD * h + HD] for c, h in chunk_blocks(heads)], axis=1)


def unpack_columns(chunks):
    place = {}
    for heads, packed in zip(CHUNKS, chunks):
        for i, block in enumerate(chunk_blocks(heads)):
            place[block] = packed[:, HD * i:HD * i + HD]
    parts = [jnp.concatenate([place[c, h] for h in range(len(KEY_UPPER))], axis=1) for c in range(3)]
    return jnp.stack(parts, axis=1)


def plane_groups(groups):
    return [list(range(first, groups, 2)) for first in range(2)]


def swap_pair(block):
    groups = lax.axis_size("dp")
    return lax.ppermute(block, "dp", [(i, i ^ 1) for i in range(groups)])


def spread_plane(block):
    return jnp.broadcast_to(block[None], (lax.axis_size("dp") // 2,) + block.shape)


def gather_plane(spread):
    groups = lax.axis_size("dp")
    got = lax.all_to_all(spread, "dp", 0, 0, axis_index_groups=plane_groups(groups), tiled=True)
    return got.reshape(got.shape[0] * got.shape[1], got.shape[2])


def exchange_terms(term):
    groups = lax.axis_size("dp")
    return lax.all_to_all(
        term.reshape(groups // 2, term.shape[0] * 2 // groups, term.shape[1]), "dp", 0, 0,
        axis_index_groups=plane_groups(groups), tiled=True,
    )


def sum_terms(terms):
    second = lax.axis_index("dp") % 2
    total = jnp.sum(terms.astype(F32), axis=0)
    halves = total.reshape(2, total.shape[0] // 2, total.shape[1])
    keep = lax.dynamic_index_in_dim(halves, second, 0, keepdims=False)
    give = lax.dynamic_index_in_dim(halves, 1 - second, 0, keepdims=False)
    got = swap_pair(give.astype(BF16))
    return keep + got.astype(F32)


def grad_tiles(out_grad):
    empty = jnp.zeros((out_grad.shape[0], HD), out_grad.dtype)
    return jnp.concatenate([out_grad[:, :256], empty, out_grad[:, 256:]], axis=1)


FRAME_SIDE = [(0, 2), (1, 3), (2, 0), (3, 1)]
FRAME_CORE = [(0, 1), (1, 0), (2, 3), (3, 2)]


def swap_side(block):
    return lax.ppermute(block, "frame", FRAME_SIDE)


def swap_core(block):
    return lax.ppermute(block, "frame", FRAME_CORE)


def per_device(
    hidden_in, rec_lengths, token_positions, thinker_grad, norm_gain, norm_bias, qkv_weight
):
    head_cols = qkv_weight.shape[2]
    think_rows = thinker_grad.shape[0]
    place = lax.axis_index("frame")
    side, core = place // 2, place % 2
    shard = jnp.concatenate([pack_columns(qkv_weight, heads) for heads in CHUNKS], axis=1)
    other = swap_pair(shard)
    both = jnp.where(lax.axis_index("dp") % 2 == 0, jnp.concatenate([shard, other]), jnp.concatenate([other, shard]))
    cut = HD * len(chunk_blocks(CHUNKS[0]))
    shards = [spread_plane(both[:, :cut])]
    shards.append(spread_plane(both[:, cut:]))
    weights = [gather_plane(shards[0])]
    own, standard, inv_std = norm_forward(hidden_in, norm_gain, norm_bias)
    far = swap_side(own)
    near = swap_core(own)
    sides = [lax.dynamic_slice_in_dim(thinker_grad, 2 * head_cols * at, 2 * head_cols, 1) for at in (side, 1 - side)]
    far_think = swap_side(sides[1])
    cols = lambda block, at: lax.dynamic_slice_in_dim(block, head_cols * at, head_cols, 1)
    near_half, own_half = cols(sides[0], 1 - core), cols(sides[0], core)
    near_think = swap_core(near_half)
    far_near = swap_core(far)
    far_near_think = swap_core(cols(far_think, 1 - core))
    shard, weights[0] = lax.optimization_barrier((shards[1], weights[0]))
    weights.append(gather_plane(shard))
    moved = jnp.concatenate([own_half, near_think, cols(far_think, core), far_near_think], axis=0)
    rows_at = ((token_positions // think_rows) ^ place) * think_rows + token_positions % think_rows
    out_grad = grad_tiles(jnp.take(moved, rows_at, axis=0, mode="clip"))
    pieces = (own, near, far, far_near)
    at = place.reshape(1)
    grads, terms = [], []
    for n, (heads, weight) in enumerate(zip(CHUNKS, weights)):
        before = (grads[0], weights[0]) if n else ()
        grad, term, *far_sums = attention(heads, rec_lengths[0], at, pieces, weight, out_grad, before)
        grads.append(grad)
        terms.append(exchange_terms(term))
    keep, give = far_sums
    got = swap_core(give)
    side_sum = swap_side((keep + got.astype(F32)).astype(BF16))
    keep, give = norm_grad_blocks(0, 1, at, grads, weights)
    core_sum = swap_core(give)
    norm_grad = keep + core_sum.astype(F32) + side_sum.astype(F32)
    weight_grad = unpack_columns([sum_terms(term) for term in terms])
    hidden_grad = norm_backward(norm_grad, standard, inv_std, norm_gain)
    return (hidden_grad, weight_grad)


def solution(mesh):
    placed = (
        P(("dp", "frame"), None),
        P("dp", None),
        P("dp"),
        P(("dp", "frame"), None),
        P(),
        P(),
        P("dp", None, "frame"),
    )

    return jax.shard_map(
        per_device,
        mesh=mesh,
        in_specs=placed,
        out_specs=(P(("dp", "frame"), None), P("dp", None, "frame")),
        check_vma=False,
    )
```
